32 devices in a mesh: row: 8 (over z, core), col: 4 (over y, x).
Axes of the slice: x: 2, y: 2, z: 4, core: 2. Of those that a mesh axis runs over, the one named last changes fastest.
Arguments:
- local_gap: bfloat16 [8, 4, 112, 4, 224], P('row', 'col')
- dual_ops: bfloat16 [8, 4, 896, 896], P('row', 'col'), as said below
- geneo_modes: bfloat16 [8, 4, 128, 896], P('row', 'col'), may hold values from -0.1875 to 0.1875
- coarse_inverse: float32 [8, 512, 512], P('row', 'col'), as said below
- face_rows: int32 [8, 4, 4], P('row', 'col'), may hold values from 0 to 224, as said below
Outputs:
- solution: float32 [8, 4, 112, 4, 224], P('row', 'col')
The draws below stay inside these ranges and needn't reach their ends.
Inputs may be any that keep to these rules, and one draw needn't show every extreme that they name: face_rows[i, j, f] counts the live dual rows of face f (north, south, west, east) of subdomain (i, j); faces on the outer edge of the grid have 0, every other face 224 // 2 or more; the two subdomains sharing a face give it the same count; some face has 224. `dual_ops`: each subdomain's dual operator is symmetric positive definite. `coarse_inverse`: each strip's coarse inverse is exactly symmetric.
All inputs are finite; a program needn't handle non-finite values.
Results may differ from the reference program's by a relative error of at most 0.003.
Values sent between devices are 32-bit elements; how exact they have to be, the bound alone decides.
No kernel may reach another device: no remote copies, remote signals or barrier semaphores. Data moves between devices by JAX's collectives and lax.ppermute only.
A program may use at most 64 MiB of HBM per device.

```python
import math
import jax
import jax.numpy as jnp
from jax import lax

FD = 224
M = 896
NM = 128
K = 112
ITERS = 2
GR = 8
GC = 4
CO = 512


stiff_log_range = math.log(10.0)


def stiffness_field(key):
    logs = jax.random.uniform(jax.random.fold_in(key, 71), (GR, GC), jnp.float32, -stiff_log_range, stiff_log_range)
    return logs


def draw_local_gap(key, part):
    keys = jax.random.split(jax.random.fold_in(key, 11), 4)
    row_pos = lax.broadcasted_iota(jnp.float32, (GR, GC), 0)
    col_pos = lax.broadcasted_iota(jnp.float32, (GR, GC), 1)
    order = (row_pos * GC + col_pos) / max(GR * GC - 1, 1)
    rising = jnp.sqrt(1.0 + 2.0 * order)
    stiff_logs = stiffness_field(key)
    exponents = jax.random.uniform(keys[3], (K,), jnp.float32, -0.5, 0.5)
    spread_arg = 2.0 * exponents * stiff_log_range
    small_arg = jnp.abs(spread_arg) < 0.001
    safe_arg = jnp.where(small_arg, 1.0, spread_arg)
    moment = jnp.where(small_arg, 1.0 + spread_arg * spread_arg / 6.0, jnp.sinh(safe_arg) / safe_arg)
    column_weight = jnp.exp(stiff_logs[:, :, None] * exponents[None, None, :]) / jnp.sqrt(moment)[None, None, :]
    values = jax.random.normal(keys[0], (GR, GC, K, 4, FD), jnp.float32)
    values = values * column_weight[:, :, :, None, None]
    return (values * rising[:, :, None, None, None]).astype(jnp.bfloat16)


def draw_dual_ops(key, part):
    base_key = jax.random.fold_in(key, 23)
    stiffness = jnp.exp(stiffness_field(key)).reshape(GR * GC)

    def one_block(operands):
        index = operands[0]
        factor_scale = operands[1]
        sub_key = jax.random.fold_in(base_key, index)
        keys = jax.random.split(sub_key, 2)
        factor = jax.random.normal(keys[0], (M, M), jnp.float32)
        gram = jnp.dot(factor, factor.T) / M
        gram = 0.5 * (gram + gram.T)
        diagonal = jax.random.uniform(keys[1], (M,), jnp.float32, 0.5, 2.0)
        block = gram + jnp.diag(diagonal)
        return (block * factor_scale).astype(jnp.bfloat16)
    blocks = lax.map(one_block, (jnp.arange(GR * GC, dtype=jnp.int32), stiffness))
    return blocks.reshape(GR, GC, M, M)


def draw_coarse_inverse(key, part):
    base_key = jax.random.fold_in(key, 37)

    def one_strip(index):
        keys = jax.random.split(jax.random.fold_in(base_key, index), 2)
        raw = jax.random.normal(keys[0], (CO, CO), jnp.float32)
        sym = (raw + raw.T) * (0.4 / math.sqrt(2.0 * CO))
        diagonal = jax.random.uniform(keys[1], (CO,), jnp.float32, 0.6, 1.4)
        return sym + jnp.diag(diagonal)
    return lax.map(one_strip, jnp.arange(GR, dtype=jnp.int32))


def draw_face_rows(key, part):
    owned = jax.random.randint(jax.random.fold_in(key, 53), (GR, GC, 2), FD // 2, FD + 1).astype(jnp.int32)
    owned = owned.at[0, 0, 0].set(FD)
    owned = owned.at[0, 0, 1].set(FD)
    row_pos = lax.broadcasted_iota(jnp.int32, (GR, GC), 0)
    col_pos = lax.broadcasted_iota(jnp.int32, (GR, GC), 1)
    south_face = jnp.where(row_pos < GR - 1, owned[:, :, 0], 0)
    east_face = jnp.where(col_pos < GC - 1, owned[:, :, 1], 0)
    north_face = jnp.concatenate([jnp.zeros((1, GC), jnp.int32), south_face[:-1]], axis=0)
    west_face = jnp.concatenate([jnp.zeros((GR, 1), jnp.int32), east_face[:, :-1]], axis=1)
    return jnp.stack([north_face, south_face, west_face, east_face], axis=2).astype(jnp.int32)


def block_scale(key, extent, cuts, low, largest):
    level, own = 1.0, jax.random.fold_in(key, 6)
    for dim, blocks in cuts:
        draws = jnp.exp(jax.random.uniform(jax.random.fold_in(own, dim), (blocks,), jnp.float32, low / len(cuts), largest / len(cuts)))
        level = level * jnp.repeat(draws, extent[dim] // blocks).reshape([-1 if axis == dim else 1 for axis in range(len(extent))])
    return level


def gaussian(stream_key, dims, spread, reach, pieces=(), kind=jnp.bfloat16):
    level = block_scale(stream_key, dims, pieces, -0.22, 0.18) if pieces else 1.0
    result = jax.random.normal(stream_key, dims, jnp.float32) * spread * level
    return jnp.minimum(jnp.maximum(result, -reach), reach).astype(kind)


def setup_inputs(seed: int = 0) -> dict:
    key_of = jax.random.split(jax.random.key(seed), 6)
    local_gap = draw_local_gap(jax.random.fold_in(key_of[5], 71), 0)
    dual_ops = draw_dual_ops(jax.random.fold_in(key_of[5], 71), 0)
    geneo_modes = gaussian(key_of[2], (GR, GC, NM, M), M ** -0.5, 0.1875, ((0, 8), (1, 4)))
    coarse_inverse = draw_coarse_inverse(jax.random.fold_in(key_of[5], 71), 0)
    face_rows = draw_face_rows(jax.random.fold_in(key_of[5], 71), 0)
    return dict(local_gap=local_gap, dual_ops=dual_ops, geneo_modes=geneo_modes, coarse_inverse=coarse_inverse, face_rows=face_rows)


face_sign_values = (-1.0, 1.0, -1.0, 1.0)


def sign_array():
    return jnp.array(face_sign_values, jnp.float32).reshape(1, 1, 1, 4, 1)


def face_live(face_rows):
    rows_iota = lax.broadcasted_iota(jnp.int32, (1, 1, 1, 1, FD), 4)
    return (rows_iota < face_rows[:, :, None, :, None]).astype(jnp.float32)


def glue_faces(local_part, live_mask):
    zero_row = jnp.zeros_like(local_part[:1, :, :, 0])
    zero_col = jnp.zeros_like(local_part[:, :1, :, 0])
    north_face = local_part[:, :, :, 0] + jnp.concatenate([zero_row, local_part[:-1, :, :, 1]], axis=0)
    south_face = local_part[:, :, :, 1] + jnp.concatenate([local_part[1:, :, :, 0], zero_row], axis=0)
    west_face = local_part[:, :, :, 2] + jnp.concatenate([zero_col, local_part[:, :-1, :, 3]], axis=1)
    east_face = local_part[:, :, :, 3] + jnp.concatenate([local_part[:, 1:, :, 2], zero_col], axis=1)
    return jnp.stack([north_face, south_face, west_face, east_face], axis=3) * live_mask


def subdomain_product(operands):
    return jnp.dot(operands[0], operands[1], preferred_element_type=jnp.float32)


def apply_dual(vector, dual_ops, live_mask):
    signed = (vector * sign_array()).astype(jnp.bfloat16).reshape(GR * GC, K, M)
    images = lax.map(subdomain_product, (signed, dual_ops.reshape(GR * GC, M, M)))
    return glue_faces(images.reshape(GR, GC, K, 4, FD) * sign_array(), live_mask)


def mode_terms(operands):
    return lax.dot_general(operands[0], operands[1], (((1,), (1,)), ((), ())), preferred_element_type=jnp.float32)


def coarse_rows(operands):
    return jnp.dot(operands[0], operands[1], precision=lax.Precision.HIGHEST, preferred_element_type=jnp.float32)


def spread_modes(operands):
    return lax.dot_general(operands[0], operands[1], (((0,), (0,)), ((), ())), preferred_element_type=jnp.float32)


def project(vector, geneo_modes, coarse_inverse, live_mask):
    rounded = vector.astype(jnp.bfloat16).reshape(GR * GC, K, M)
    flat_modes = geneo_modes.reshape(GR * GC, NM, M)
    mode_coeffs = lax.map(mode_terms, (flat_modes, rounded)).reshape(GR, CO, K)
    coarse_values = lax.map(coarse_rows, (coarse_inverse, mode_coeffs))
    coarse_values = coarse_values.astype(jnp.bfloat16).reshape(GR * GC, NM, K)
    local_part = lax.map(spread_modes, (coarse_values, flat_modes))
    return vector - glue_faces(local_part.reshape(GR, GC, K, 4, FD), live_mask)


def inner_product(left_side, right_side):
    return 0.5 * jnp.sum(left_side * right_side, axis=(0, 1, 3, 4))


def reference(local_gap, dual_ops, geneo_modes, coarse_inverse, face_rows):
    live_mask = face_live(face_rows)
    residual = glue_faces(local_gap.astype(jnp.float32) * sign_array(), live_mask)
    projected = project(residual, geneo_modes, coarse_inverse, live_mask)
    norm_now = inner_product(projected, projected)
    direction = projected
    solution = jnp.zeros_like(residual)
    for iteration in range(ITERS):
        image = apply_dual(direction, dual_ops, live_mask)
        step_size = (norm_now / inner_product(direction, image)).reshape(1, 1, K, 1, 1)
        solution = solution + step_size * direction
        if iteration + 1 < ITERS:
            residual = residual - step_size * image
            projected = project(residual, geneo_modes, coarse_inverse, live_mask)
            norm_next = inner_product(projected, projected)
            direction = projected + (norm_next / norm_now).reshape(1, 1, K, 1, 1) * direction
            norm_now = norm_next
    return solution
```

```python
import jax
import jax.numpy as jnp
from jax import lax
from jax.sharding import PartitionSpec as P

FACE_SIGNS = (-1.0, 1.0, -1.0, 1.0)


def swap_tables(rows, cols):
    def table(partner):
        pairs = []
        for r in range(rows):
            for c in range(cols):
                r2, c2 = partner(r, c)
                pairs.append((r * cols + c, r2 * cols + c2))
        return pairs

    def across_rows(r, c):
        other = r + 1 if r % 2 else r - 1
        return (other, c) if 0 <= other < rows else (r, c ^ 1)

    def across_cols(r, c):
        other = c + 1 if c % 2 else c - 1
        return r, other % cols

    return dict(
        mate_row=table(lambda r, c: (r ^ 1, c)),
        next_row=table(across_rows),
        mate_col=table(lambda r, c: (r, c ^ 1)),
        next_col=table(across_cols),
    )


def swap(value, pairs):
    return lax.ppermute(value, ("row", "col"), pairs)


def exchange(field, tables, odd_row, odd_col):
    north, south, west, east = field
    got_mate_row = swap(jnp.where(odd_row, north, south), tables["mate_row"])
    got_next_row = swap(jnp.where(odd_row, south, north), tables["next_row"])
    got_mate_col = swap(jnp.where(odd_col, west, east), tables["mate_col"])
    got_next_col = swap(jnp.where(odd_col, east, west), tables["next_col"])
    return jnp.stack(
        [
            north + jnp.where(odd_row, got_mate_row, got_next_row),
            south + jnp.where(odd_row, got_next_row, got_mate_row),
            west + jnp.where(odd_col, got_mate_col, got_next_col),
            east + jnp.where(odd_col, got_next_col, got_mate_col),
        ]
    )


def gather_strip(block, cols):
    mine = lax.axis_index("col")
    parts = [block]
    for step in range(1, cols):
        parts.append(lax.ppermute(block, "col", [(c, c ^ step) for c in range(cols)]))
    parts = jnp.stack(parts)
    return jnp.concatenate([parts[mine ^ c] for c in range(cols)], axis=0)


def on_device(rows, cols, local_gap, dual_ops, geneo_modes, coarse_inverse, face_rows):
    tables = swap_tables(rows, cols)
    odd_row = lax.axis_index("row") % 2 == 1
    odd_col = lax.axis_index("col") % 2 == 1
    operator = dual_ops[0, 0]
    modes = geneo_modes[0, 0]
    coarse_block = coarse_inverse[0]
    unknowns = operator.shape[0]
    columns, faces, depth = local_gap.shape[2:]
    sign = jnp.array(FACE_SIGNS, jnp.float32).reshape(faces, 1, 1)
    live = lax.broadcasted_iota(jnp.int32, (faces, depth, 1), 1) < face_rows[0, 0][:, None, None]

    def glue(field):
        return jnp.where(live, exchange(field, tables, odd_row, odd_col), 0.0)

    def flat(field):
        return field.astype(jnp.bfloat16).reshape(unknowns, columns)

    def apply_dual(vector):
        image = jnp.dot(operator, flat(vector * sign), preferred_element_type=jnp.float32)
        return image.reshape(vector.shape) * sign

    def coarse_part(vector):
        coeffs = jnp.dot(modes, flat(vector), preferred_element_type=jnp.float32)
        return coeffs

    def spread(coeffs):
        coarse = jnp.dot(
            coarse_block, coeffs, precision=lax.Precision.HIGHEST, preferred_element_type=jnp.float32
        )
        part = lax.dot_general(
            modes, coarse.astype(jnp.bfloat16), (((0,), (0,)), ((), ())), preferred_element_type=jnp.float32
        )
        return part.reshape(faces, depth, columns)

    gap = jnp.transpose(local_gap[0, 0], (1, 2, 0)).astype(jnp.float32) * sign
    residual = glue(gap)
    first = residual - glue(spread(gather_strip(coarse_part(residual), cols)))
    first_image = apply_dual(first)
    image = glue(first_image)
    second = image - glue(spread(gather_strip(coarse_part(image), cols)))
    second_image = apply_dual(second)

    def inner(left, right):
        return jnp.sum(left * right, axis=(0, 1))

    partial = jnp.stack(
        [
            0.5 * inner(first, first),
            inner(first, first_image),
            0.5 * inner(first, second),
            0.5 * inner(second, second),
            inner(first, second_image) + inner(second, first_image),
            inner(second, second_image),
        ]
    )
    devices = rows * cols
    every = lax.all_to_all(jnp.broadcast_to(partial[None], (devices,) + partial.shape), ("row", "col"), 0, 0)
    norm, curvature, mixed, square, cross, bend = jnp.sum(every, axis=0)
    step = norm / curvature
    fresh = norm - 2.0 * step * mixed + step * (step * square)
    ratio = fresh / norm
    grow = 1.0 + ratio
    next_curvature = grow * (grow * curvature) - grow * (step * cross) + step * (step * bend)
    next_step = fresh / next_curvature
    solution = (step + next_step * grow) * first - (next_step * step) * second
    return jnp.transpose(solution, (2, 0, 1))[None, None]


def solution(mesh):
    rows, cols = mesh.shape["row"], mesh.shape["col"]

    def body(*arrays):
        return on_device(rows, cols, *arrays)

    return jax.shard_map(
        body,
        mesh=mesh,
        in_specs=(
            P("row", "col", None, None, None),
            P("row", "col", None, None),
            P("row", "col", None, None),
            P("row", "col", None),
            P("row", "col", None),
        ),
        out_specs=P("row", "col", None, None, None),
        check_vma=False,
    )
```

```python
import functools

import jax
import jax.numpy as jnp
from jax import lax
from jax.experimental import pallas as pl
from jax.experimental.pallas import tpu as pltpu
from jax.sharding import PartitionSpec as P

PARTNERS = 4
SCALE_ROWS = 8


def swap_tables(rows, cols):
    def table(partner):
        pairs = []
        for r in range(rows):
            for c in range(cols):
                r2, c2 = partner(r, c)
                pairs.append((r * cols + c, r2 * cols + c2))
        return pairs

    def across_rows(r, c):
        other = r + 1 if r % 2 else r - 1
        return (other, c) if 0 <= other < rows else (r, c ^ 1)

    def across_cols(r, c):
        other = c + 1 if c % 2 else c - 1
        return r, other % cols

    return [
        table(lambda r, c: (r ^ 1, c)),
        table(across_rows),
        table(lambda r, c: (r, c ^ 1)),
        table(across_cols),
    ]


def faces_of_partners():
    odd_row = lax.rem(lax.axis_index("row"), 2)
    odd_col = lax.rem(lax.axis_index("col"), 2)
    return [1 - odd_row, odd_row, 3 - odd_col, 2 + odd_col]


def face_slice(face, depth):
    return pl.ds(pl.multiple_of(face * depth, depth), depth)


def face_sign(face):
    return (2 * lax.rem(face, 2) - 1).astype(jnp.float32)


def masked(value, count):
    unknown = lax.broadcasted_iota(jnp.int32, value.shape, 0)
    return jnp.where(unknown < count, value, 0.0)


def column_sum(value):
    return jnp.sum(value, axis=0, keepdims=True)


def gap_kernel(gap_ref, *refs):
    out_refs, field = refs[:PARTNERS], refs[PARTNERS]
    depth = gap_ref.shape[2]
    for face in range(PARTNERS):
        sign = 1.0 if face % 2 else -1.0
        block = gap_ref[:, face, :].astype(jnp.float32) * sign
        field[face * depth : (face + 1) * depth, :] = block.T
    for face, out_ref in zip(faces_of_partners(), out_refs):
        out_ref[...] = field[face_slice(face, depth), :]


def turn_kernel(modes_ref, out_ref):
    out_ref[...] = modes_ref[...].astype(jnp.float32).T.astype(jnp.bfloat16)


def read_pair(mine_ref, got_ref, count, scaled):
    depth = mine_ref.shape[0] - (SCALE_ROWS if scaled else 0)
    return mine_ref[:depth, :], got_ref[:depth, :]


def scale_of(ref):
    depth = ref.shape[0] - SCALE_ROWS
    return ref[depth : depth + 1, :]


def widest(own_scale, got_refs, counts):
    top = own_scale
    for ref, count in zip(got_refs, counts):
        top = jnp.maximum(top, jnp.where(count > 0, scale_of(ref), own_scale))
    return top


def glued(mine_refs, got_refs, counts, scaled):
    fields = []
    if scaled:
        own_scale = scale_of(mine_refs[0])
        top = widest(own_scale, got_refs, counts)
        own_factor = own_scale / top
    else:
        top = None
    for mine_ref, got_ref, count in zip(mine_refs, got_refs, counts):
        mine, got = read_pair(mine_ref, got_ref, count, scaled)
        if scaled:
            mine, got = mine * own_factor, got * (scale_of(got_ref) / top)
        fields.append(masked(mine + got, count))
    return fields, top


def counts_of(rows_ref, faces):
    return [rows_ref[0, 0, face] for face in faces]


def coeffs_kernel(scaled, rows_ref, modes_ref, *refs):
    mine_refs, got_refs, out_ref, flat = refs[:4], refs[4:8], refs[8], refs[9]
    faces = faces_of_partners()
    fields, top = glued(mine_refs, got_refs, counts_of(rows_ref, faces), scaled)
    depth = fields[0].shape[0]
    for face, field in zip(faces, fields):
        flat[face_slice(face, depth), :] = field.astype(jnp.bfloat16)
    count = modes_ref.shape[0]
    out_ref[:count, :] = jnp.dot(modes_ref[...], flat[...], preferred_element_type=jnp.float32)
    if scaled:
        out_ref[count:, :] = jnp.broadcast_to(top, (SCALE_ROWS, top.shape[1]))


def coarse_kernel(cols, scaled, coarse_ref, turned_ref, *refs):
    block_refs, out_refs = refs[:cols], refs[cols:]
    mine = lax.axis_index("col")
    count = coarse_ref.shape[0]
    depth = turned_ref.shape[0] // PARTNERS
    top = None
    if scaled:
        top = functools.reduce(jnp.maximum, [scale_of(ref) for ref in block_refs])
    total = None
    for step, ref in enumerate(block_refs):
        block = ref[:count, :]
        if scaled:
            block = block * (scale_of(ref) / top)
        start = pl.multiple_of((mine ^ step) * count, count)
        term = jnp.dot(
            coarse_ref[:, pl.ds(start, count)],
            block,
            precision=lax.Precision.HIGHEST,
            preferred_element_type=jnp.float32,
        )
        total = term if total is None else total + term
    coarse = total.astype(jnp.bfloat16)
    for face, out_ref in zip(faces_of_partners(), out_refs):
        out_ref[:depth, :] = jnp.dot(turned_ref[face_slice(face, depth), :], coarse, preferred_element_type=jnp.float32)
        if scaled:
            out_ref[depth:, :] = jnp.broadcast_to(top, (SCALE_ROWS, top.shape[1]))


def apply_dual(operator_ref, fields, faces, flat, image):
    depth = fields[0].shape[0]
    for face, field in zip(faces, fields):
        flat[face_slice(face, depth), :] = (field * face_sign(face)).astype(jnp.bfloat16)
    image[...] = jnp.dot(operator_ref[...], flat[...], preferred_element_type=jnp.float32)
    return [image[face_slice(face, depth), :] * face_sign(face) for face in faces]


def first_kernel(rows_ref, operator_ref, *refs):
    mine_refs, got_refs, part_refs, got_part_refs = refs[:4], refs[4:8], refs[8:12], refs[12:16]
    vector_refs, image_refs, sums_ref, flat, image = refs[16:20], refs[20:24], refs[24], refs[25], refs[26]
    faces = faces_of_partners()
    counts = counts_of(rows_ref, faces)
    residuals, _ = glued(mine_refs, got_refs, counts, False)
    parts, _ = glued(part_refs, got_part_refs, counts, False)
    fields = [residual - part for residual, part in zip(residuals, parts)]
    for ref, field in zip(vector_refs, fields):
        ref[...] = field
    images = apply_dual(operator_ref, fields, faces, flat, image)
    largest = jnp.max(jnp.abs(image[...]), axis=0, keepdims=True)
    largest = jnp.where(largest > 0.0, largest, 1.0)
    inverse = 1.0 / largest
    depth = fields[0].shape[0]
    norm, curvature = 0.0, 0.0
    for ref, field, value in zip(image_refs, fields, images):
        norm += column_sum(field * field)
        curvature += column_sum(field * value)
        ref[:depth, :] = value * inverse
        ref[depth:, :] = jnp.broadcast_to(largest, (SCALE_ROWS, largest.shape[1]))
    sums_ref[0:1, :] = 0.5 * norm
    sums_ref[1:2, :] = curvature


def second_kernel(rows_ref, operator_ref, sums_in_ref, *refs):
    mine_refs, got_refs, part_refs, got_part_refs, first_refs = (refs[4 * i : 4 * i + 4] for i in range(5))
    vector_refs, sums_ref, flat, image = refs[20:24], refs[24], refs[25], refs[26]
    faces = faces_of_partners()
    counts = counts_of(rows_ref, faces)
    images, image_scale = glued(mine_refs, got_refs, counts, True)
    parts, part_scale = glued(part_refs, got_part_refs, counts, True)
    top = jnp.maximum(image_scale, part_scale)
    fields = [value * (image_scale / top) - part * (part_scale / top) for value, part in zip(images, parts)]
    for ref, field in zip(vector_refs, fields):
        ref[...] = field
    own_scale = scale_of(mine_refs[0])
    depth = fields[0].shape[0]
    second_images = apply_dual(operator_ref, fields, faces, flat, image)
    mixed, square, cross, bend = 0.0, 0.0, 0.0, 0.0
    reach = 0.0
    for first_ref, mine_ref, field, value in zip(first_refs, mine_refs, fields, second_images):
        first = first_ref[...]
        mixed += column_sum(first * field)
        square += column_sum(field * field)
        cross += column_sum(first * value)
        reach += column_sum(field * mine_ref[:depth, :])
        bend += column_sum(field * value)
    rows = [sums_in_ref[0:1, :], sums_in_ref[1:2, :], 0.5 * mixed, 0.5 * square, cross + own_scale * reach, bend, top, top]
    table = jnp.concatenate(rows, axis=0)
    sums_ref[...] = jnp.broadcast_to(table[None], sums_ref.shape)


def last_kernel(sums_ref, *refs):
    first_refs, second_refs, out_ref, field = refs[:4], refs[4:8], refs[8], refs[9]
    faces = faces_of_partners()
    device = lax.axis_index("row") * lax.axis_size("col") + lax.axis_index("col")
    every = sums_ref[...]
    scales = every[:, 6:7, :]
    top = jnp.max(scales, axis=0, keepdims=True)
    share = scales / top
    norm = jnp.sum(every[:, 0:1, :], axis=0)
    curvature = jnp.sum(every[:, 1:2, :], axis=0)
    mixed = jnp.sum(every[:, 2:3, :] * share, axis=0)
    square = jnp.sum(every[:, 3:4, :] * share * share, axis=0)
    cross = jnp.sum(every[:, 4:5, :] * share, axis=0)
    bend = jnp.sum(every[:, 5:6, :] * share * share, axis=0)
    step = norm / curvature
    reach = step * top[0]
    fresh = norm - 2.0 * reach * mixed + reach * (reach * square)
    ratio = fresh / norm
    grow = 1.0 + ratio
    next_curvature = grow * (grow * curvature) - grow * (reach * cross) + reach * (reach * bend)
    next_step = fresh / next_curvature
    along_first = step + next_step * grow
    along_second = next_step * (step * sums_ref[device, 6:7, :])
    depth = first_refs[0].shape[0]
    for face, first_ref, second_ref in zip(faces, first_refs, second_refs):
        field[face_slice(face, depth), :] = along_first * first_ref[...] - along_second * second_ref[...]
    for face in range(PARTNERS):
        out_ref[:, face, :] = field[face * depth : (face + 1) * depth, :].T


VMEM = pl.BlockSpec(memory_space=pltpu.VMEM)
SMEM = pl.BlockSpec(memory_space=pltpu.SMEM)


def run(kernel, name, outs, scratch, in_specs, args, flops=0):
    moved = sum(a.size * a.dtype.itemsize for a in args)
    return pl.pallas_call(
        kernel,
        name=name,
        out_shape=outs,
        in_specs=in_specs,
        out_specs=jax.tree.map(lambda _: VMEM, outs),
        scratch_shapes=scratch,
        compiler_params=pltpu.CompilerParams(vmem_limit_bytes=16 * 2**20),
        cost_estimate=pl.CostEstimate(flops=flops, bytes_accessed=moved, transcendentals=0),
    )(*args)


def on_device(rows, cols, local_gap, dual_ops, geneo_modes, coarse_inverse, face_rows):
    tables = swap_tables(rows, cols)
    gap = local_gap[0, 0]
    operator = dual_ops[0, 0]
    modes = geneo_modes[0, 0]
    coarse_block = coarse_inverse[0]
    columns, _, depth = gap.shape
    unknowns = operator.shape[0]
    count = modes.shape[0]

    def shape(*dims, dtype=jnp.float32):
        return jax.ShapeDtypeStruct(dims, dtype)

    def swap(fields):
        return [lax.ppermute(field, ("row", "col"), pairs) for field, pairs in zip(fields, tables)]

    def gather(block):
        steps = [[(c, c ^ step) for c in range(cols)] for step in range(1, cols)]
        return [block] + [lax.ppermute(block, "col", pairs) for pairs in steps]

    def four(height):
        return [shape(height, columns)] * PARTNERS

    flat = pltpu.VMEM((unknowns, columns), jnp.bfloat16)
    wide = pltpu.VMEM((unknowns, columns), jnp.float32)
    tall = depth + SCALE_ROWS

    gaps = run(gap_kernel, "gap", four(depth), [wide], [VMEM], [gap])
    got_gaps = swap(gaps)
    turned = run(turn_kernel, "turn", shape(unknowns, count, dtype=jnp.bfloat16), [], [VMEM], [modes])
    coeffs = run(
        functools.partial(coeffs_kernel, False), "coeffs", shape(count, columns), [flat],
        [SMEM] + [VMEM] * 9, [face_rows, modes, *gaps, *got_gaps],
    )
    parts = run(
        functools.partial(coarse_kernel, cols, False), "coarse", four(depth), [],
        [VMEM] * (2 + cols), [coarse_block, turned, *gather(coeffs)],
    )
    got_parts = swap(parts)
    *first, sums = run(
        first_kernel, "first", four(depth) + four(tall) + [shape(2, columns)], [flat, wide],
        [SMEM] + [VMEM] * 17, [face_rows, operator, *gaps, *got_gaps, *parts, *got_parts],
    )
    first, images = first[:PARTNERS], first[PARTNERS:]
    got_images = swap(images)
    coeffs = run(
        functools.partial(coeffs_kernel, True), "coeffs2", shape(count + SCALE_ROWS, columns), [flat],
        [SMEM] + [VMEM] * 9, [face_rows, modes, *images, *got_images],
    )
    parts = run(
        functools.partial(coarse_kernel, cols, True), "coarse2", four(tall), [],
        [VMEM] * (2 + cols), [coarse_block, turned, *gather(coeffs)],
    )
    got_parts = swap(parts)
    *second, sums = run(
        second_kernel, "second", four(depth) + [shape(rows * cols, 8, columns)], [flat, wide],
        [SMEM] + [VMEM] * 22, [face_rows, operator, sums, *images, *got_images, *parts, *got_parts, *first],
    )
    every = lax.all_to_all(sums, ("row", "col"), 0, 0)
    out = run(
        last_kernel, "last", shape(columns, PARTNERS, depth), [wide],
        [VMEM] * 9, [every, *first, *second],
    )
    return out[None, None]


def solution(mesh):
    rows, cols = mesh.shape["row"], mesh.shape["col"]

    def body(*arrays):
        return on_device(rows, cols, *arrays)

    return jax.shard_map(
        body,
        mesh=mesh,
        in_specs=(
            P("row", "col", None, None, None),
            P("row", "col", None, None),
            P("row", "col", None, None),
            P("row", "col", None),
            P("row", "col", None),
        ),
        out_specs=P("row", "col", None, None, None),
        check_vma=False,
    )
```

```python
import functools

import jax
import jax.numpy as jnp
from jax import lax
from jax.experimental import pallas as pl
from jax.experimental.pallas import tpu as pltpu
from jax.sharding import PartitionSpec as P

PARTNERS = 4
SCALE_ROWS = 8


def swap_tables(rows, cols):
    def table(partner):
        pairs = []
        for r in range(rows):
            for c in range(cols):
                r2, c2 = partner(r, c)
                pairs.append((r * cols + c, r2 * cols + c2))
        return pairs

    idle = 2 if cols % 4 == 0 else 1

    def across_rows(r, c):
        other = r + 1 if r % 2 else r - 1
        return (other, c) if 0 <= other < rows else (r, c ^ idle)

    def across_cols(r, c):
        other = c + 1 if c % 2 else c - 1
        return (r, other) if 0 <= other < cols else (r ^ 1, c)

    return [
        table(across_cols),
        table(lambda r, c: (r, c ^ 1)),
        table(across_rows),
        table(lambda r, c: (r ^ 1, c)),
    ]


def faces_of_partners():
    odd_row = lax.rem(lax.axis_index("row"), 2)
    odd_col = lax.rem(lax.axis_index("col"), 2)
    return [2 + odd_col, 3 - odd_col, odd_row, 1 - odd_row]


def face_slice(face, depth):
    return pl.ds(pl.multiple_of(face * depth, depth), depth)


def face_sign(face):
    return (2 * lax.rem(face, 2) - 1).astype(jnp.float32)


def masked(value, count):
    unknown = lax.broadcasted_iota(jnp.int32, value.shape, 0)
    return jnp.where(unknown < count, value, 0.0)


def column_sum(value):
    return jnp.sum(value, axis=0, keepdims=True)


def gap_kernel(gap_ref, *refs):
    out_refs, field = refs[:PARTNERS], refs[PARTNERS]
    depth = gap_ref.shape[2]
    for face in range(PARTNERS):
        sign = 1.0 if face % 2 else -1.0
        block = gap_ref[:, face, :].astype(jnp.float32) * sign
        field[face * depth : (face + 1) * depth, :] = block.T
    for face, out_ref in zip(faces_of_partners(), out_refs):
        out_ref[...] = field[face_slice(face, depth), :]


def prepare_kernel(rows_hbm, modes_hbm, coarse_hbm, after_ref, counts_ref, modes_ref, coarse_ref, turned_ref, rows, sems):
    del after_ref
    copies = [
        pltpu.make_async_copy(rows_hbm, rows, sems.at[0]),
        pltpu.make_async_copy(modes_hbm, modes_ref, sems.at[1]),
        pltpu.make_async_copy(coarse_hbm, coarse_ref, sems.at[2]),
    ]
    for copy in copies:
        copy.start()
    copies[0].wait()
    for partner, face in enumerate(faces_of_partners()):
        counts_ref[partner : partner + 1, :] = jnp.full((1, counts_ref.shape[1]), rows[0, 0, face], jnp.int32)
    copies[1].wait()
    turned_ref[...] = modes_ref[...].astype(jnp.float32).T.astype(jnp.bfloat16)
    copies[2].wait()


def read_pair(mine_ref, got_ref, count, scaled):
    depth = mine_ref.shape[0] - (SCALE_ROWS if scaled else 0)
    return mine_ref[:depth, :], got_ref[:depth, :]


def scale_of(ref):
    depth = ref.shape[0] - SCALE_ROWS
    return ref[depth : depth + 1, :]


def widest(own_scale, got_refs, counts):
    top = own_scale
    for ref, count in zip(got_refs, counts):
        top = jnp.maximum(top, jnp.where(count > 0, scale_of(ref), own_scale))
    return top


def glued(mine_refs, got_refs, counts, scaled):
    fields = []
    if scaled:
        own_scale = scale_of(mine_refs[0])
        top = widest(own_scale, got_refs, counts)
        own_factor = own_scale / top
    else:
        top = None
    for mine_ref, got_ref, count in zip(mine_refs, got_refs, counts):
        mine, got = read_pair(mine_ref, got_ref, count, scaled)
        if scaled:
            mine, got = mine * own_factor, got * (scale_of(got_ref) / top)
        fields.append(masked(mine + got, count))
    return fields, top


def counts_of(counts_ref):
    return [counts_ref[partner : partner + 1, :] for partner in range(PARTNERS)]


def coeffs_kernel(scaled, counts_ref, modes_ref, *refs):
    mine_refs, got_refs, out_ref, flat = refs[:4], refs[4:8], refs[8], refs[9]
    faces = faces_of_partners()
    fields, top = glued(mine_refs, got_refs, counts_of(counts_ref), scaled)
    depth = fields[0].shape[0]
    for face, field in zip(faces, fields):
        flat[face_slice(face, depth), :] = field.astype(jnp.bfloat16)
    count = modes_ref.shape[0]
    out_ref[:count, :] = jnp.dot(modes_ref[...], flat[...], preferred_element_type=jnp.float32)
    if scaled:
        out_ref[count:, :] = jnp.broadcast_to(top, (SCALE_ROWS, top.shape[1]))


def coarse_kernel(cols, scaled, coarse_ref, turned_ref, *refs):
    block_refs, out_refs = refs[:cols], refs[cols:]
    mine = lax.axis_index("col")
    count = coarse_ref.shape[0]
    depth = turned_ref.shape[0] // PARTNERS
    top = None
    if scaled:
        top = functools.reduce(jnp.maximum, [scale_of(ref) for ref in block_refs])
    total = None
    for step, ref in enumerate(block_refs):
        block = ref[:count, :]
        if scaled:
            block = block * (scale_of(ref) / top)
        start = pl.multiple_of((mine ^ step) * count, count)
        term = jnp.dot(
            coarse_ref[:, pl.ds(start, count)],
            block,
            precision=lax.Precision.HIGHEST,
            preferred_element_type=jnp.float32,
        )
        total = term if total is None else total + term
    coarse = total.astype(jnp.bfloat16)
    for face, out_ref in zip(faces_of_partners(), out_refs):
        out_ref[:depth, :] = jnp.dot(turned_ref[face_slice(face, depth), :], coarse, preferred_element_type=jnp.float32)
        if scaled:
            out_ref[depth:, :] = jnp.broadcast_to(top, (SCALE_ROWS, top.shape[1]))


def apply_dual(operator_ref, fields, faces, flat, image):
    depth = fields[0].shape[0]
    for face, field in zip(faces, fields):
        flat[face_slice(face, depth), :] = (field * face_sign(face)).astype(jnp.bfloat16)
    image[...] = jnp.dot(operator_ref[...], flat[...], preferred_element_type=jnp.float32)
    return [image[face_slice(face, depth), :] * face_sign(face) for face in faces]


def first_kernel(counts_ref, operator_ref, *refs):
    mine_refs, got_refs, part_refs, got_part_refs = refs[:4], refs[4:8], refs[8:12], refs[12:16]
    vector_refs, image_refs, sums_ref, flat, image = refs[16:20], refs[20:24], refs[24], refs[25], refs[26]
    faces = faces_of_partners()
    counts = counts_of(counts_ref)
    residuals, _ = glued(mine_refs, got_refs, counts, False)
    parts, _ = glued(part_refs, got_part_refs, counts, False)
    fields = [residual - part for residual, part in zip(residuals, parts)]
    for ref, field in zip(vector_refs, fields):
        ref[...] = field
    images = apply_dual(operator_ref, fields, faces, flat, image)
    largest = jnp.max(jnp.abs(image[...]), axis=0, keepdims=True)
    largest = jnp.where(largest > 0.0, largest, 1.0)
    inverse = 1.0 / largest
    depth = fields[0].shape[0]
    norm, curvature = 0.0, 0.0
    for ref, field, value in zip(image_refs, fields, images):
        norm += column_sum(field * field)
        curvature += column_sum(field * value)
        ref[:depth, :] = value * inverse
        ref[depth:, :] = jnp.broadcast_to(largest, (SCALE_ROWS, largest.shape[1]))
    sums_ref[0:1, :] = 0.5 * norm
    sums_ref[1:2, :] = curvature


def second_kernel(counts_ref, operator_ref, sums_in_ref, *refs):
    mine_refs, got_refs, part_refs, got_part_refs, first_refs = (refs[4 * i : 4 * i + 4] for i in range(5))
    vector_refs, sums_ref, flat, image = refs[20:24], refs[24], refs[25], refs[26]
    faces = faces_of_partners()
    counts = counts_of(counts_ref)
    images, image_scale = glued(mine_refs, got_refs, counts, True)
    parts, part_scale = glued(part_refs, got_part_refs, counts, True)
    top = jnp.maximum(image_scale, part_scale)
    fields = [value * (image_scale / top) - part * (part_scale / top) for value, part in zip(images, parts)]
    for ref, field in zip(vector_refs, fields):
        ref[...] = field
    own_scale = scale_of(mine_refs[0])
    depth = fields[0].shape[0]
    second_images = apply_dual(operator_ref, fields, faces, flat, image)
    mixed, square, cross, bend = 0.0, 0.0, 0.0, 0.0
    reach = 0.0
    for first_ref, mine_ref, field, value in zip(first_refs, mine_refs, fields, second_images):
        first = first_ref[...]
        mixed += column_sum(first * field)
        square += column_sum(field * field)
        cross += column_sum(first * value)
        reach += column_sum(field * mine_ref[:depth, :])
        bend += column_sum(field * value)
    rows = [sums_in_ref[0:1, :], sums_in_ref[1:2, :], 0.5 * mixed, 0.5 * square, cross + own_scale * reach, bend, top, top]
    table = jnp.concatenate(rows, axis=0)
    sums_ref[...] = jnp.broadcast_to(table[None], sums_ref.shape)


def last_kernel(sums_ref, *refs):
    first_refs, second_refs, out_ref, field = refs[:4], refs[4:8], refs[8], refs[9]
    faces = faces_of_partners()
    device = lax.axis_index("row") * lax.axis_size("col") + lax.axis_index("col")
    every = sums_ref[...]
    scales = every[:, 6:7, :]
    top = jnp.max(scales, axis=0, keepdims=True)
    share = scales / top
    norm = jnp.sum(every[:, 0:1, :], axis=0)
    curvature = jnp.sum(every[:, 1:2, :], axis=0)
    mixed = jnp.sum(every[:, 2:3, :] * share, axis=0)
    square = jnp.sum(every[:, 3:4, :] * share * share, axis=0)
    cross = jnp.sum(every[:, 4:5, :] * share, axis=0)
    bend = jnp.sum(every[:, 5:6, :] * share * share, axis=0)
    step = norm / curvature
    reach = step * top[0]
    fresh = norm - 2.0 * reach * mixed + reach * (reach * square)
    ratio = fresh / norm
    grow = 1.0 + ratio
    next_curvature = grow * (grow * curvature) - grow * (reach * cross) + reach * (reach * bend)
    next_step = fresh / next_curvature
    along_first = step + next_step * grow
    along_second = next_step * (step * sums_ref[device, 6:7, :])
    depth = first_refs[0].shape[0]
    for face, first_ref, second_ref in zip(faces, first_refs, second_refs):
        field[face_slice(face, depth), :] = along_first * first_ref[...] - along_second * second_ref[...]
    for face in range(PARTNERS):
        out_ref[:, face, :] = field[face * depth : (face + 1) * depth, :].T


VMEM = pl.BlockSpec(memory_space=pltpu.VMEM)
HBM = pl.BlockSpec(memory_space=pltpu.HBM)


def run(kernel, name, outs, scratch, in_specs, args, flops=0):
    moved = sum(a.size * a.dtype.itemsize for a in args)
    return pl.pallas_call(
        kernel,
        name=name,
        out_shape=outs,
        in_specs=in_specs,
        out_specs=jax.tree.map(lambda _: VMEM, outs),
        scratch_shapes=scratch,
        compiler_params=pltpu.CompilerParams(vmem_limit_bytes=16 * 2**20),
        cost_estimate=pl.CostEstimate(flops=flops, bytes_accessed=moved, transcendentals=0),
    )(*args)


def on_device(rows, cols, local_gap, dual_ops, geneo_modes, coarse_inverse, face_rows):
    tables = swap_tables(rows, cols)
    gap = local_gap[0, 0]
    operator = dual_ops[0, 0]
    modes = geneo_modes[0, 0]
    coarse_block = coarse_inverse[0]
    columns, _, depth = gap.shape
    unknowns = operator.shape[0]
    count = modes.shape[0]

    def shape(*dims, dtype=jnp.float32):
        return jax.ShapeDtypeStruct(dims, dtype)

    def swap(fields):
        return [lax.ppermute(field, ("row", "col"), pairs) for field, pairs in zip(fields, tables)]

    def gather(block):
        steps = [[(c, c ^ step) for c in range(cols)] for step in range(1, cols)]
        return [block] + [lax.ppermute(block, "col", pairs) for pairs in steps]

    def four(height):
        return [shape(height, columns)] * PARTNERS

    flat = pltpu.VMEM((unknowns, columns), jnp.bfloat16)
    wide = pltpu.VMEM((unknowns, columns), jnp.float32)
    tall = depth + SCALE_ROWS

    gaps = run(gap_kernel, "gap", four(depth), [wide], [VMEM], [gap])
    got_gaps = swap(gaps)
    counts, modes, coarse_block, turned = run(
        prepare_kernel, "prepare",
        [
            shape(PARTNERS, columns, dtype=jnp.int32),
            shape(*modes.shape, dtype=modes.dtype),
            shape(*coarse_block.shape),
            shape(unknowns, count, dtype=modes.dtype),
        ],
        [pltpu.SMEM(face_rows.shape, jnp.int32), pltpu.SemaphoreType.DMA((3,))],
        [HBM] * 3 + [VMEM], [face_rows, modes, coarse_block, gaps[PARTNERS - 1]],
    )
    coeffs = run(
        functools.partial(coeffs_kernel, False), "coeffs", shape(count, columns), [flat],
        [VMEM] * 10, [counts, modes, *gaps, *got_gaps],
    )
    parts = run(
        functools.partial(coarse_kernel, cols, False), "coarse", four(depth), [],
        [VMEM] * (2 + cols), [coarse_block, turned, *gather(coeffs)],
    )
    got_parts = swap(parts)
    *first, sums = run(
        first_kernel, "first", four(depth) + four(tall) + [shape(2, columns)], [flat, wide],
        [VMEM] * 18, [counts, operator, *gaps, *got_gaps, *parts, *got_parts],
    )
    first, images = first[:PARTNERS], first[PARTNERS:]
    got_images = swap(images)
    coeffs = run(
        functools.partial(coeffs_kernel, True), "coeffs2", shape(count + SCALE_ROWS, columns), [flat],
        [VMEM] * 10, [counts, modes, *images, *got_images],
    )
    parts = run(
        functools.partial(coarse_kernel, cols, True), "coarse2", four(tall), [],
        [VMEM] * (2 + cols), [coarse_block, turned, *gather(coeffs)],
    )
    got_parts = swap(parts)
    *second, sums = run(
        second_kernel, "second", four(depth) + [shape(rows * cols, 8, columns)], [flat, wide],
        [VMEM] * 23, [counts, operator, sums, *images, *got_images, *parts, *got_parts, *first],
    )
    every = lax.all_to_all(sums, ("row", "col"), 0, 0)
    out = run(
        last_kernel, "last", shape(columns, PARTNERS, depth), [wide],
        [VMEM] * 9, [every, *first, *second],
    )
    return out[None, None]


def solution(mesh):
    rows, cols = mesh.shape["row"], mesh.shape["col"]

    def body(*arrays):
        return on_device(rows, cols, *arrays)

    return jax.shard_map(
        body,
        mesh=mesh,
        in_specs=(
            P("row", "col", None, None, None),
            P("row", "col", None, None),
            P("row", "col", None, None),
            P("row", "col", None),
            P("row", "col", None),
        ),
        out_specs=P("row", "col", None, None, None),
        check_vma=False,
    )
```

```python
import functools

import jax
import jax.numpy as jnp
from jax import lax
from jax.experimental import pallas as pl
from jax.experimental.pallas import tpu as pltpu
from jax.sharding import PartitionSpec as P

PARTNERS = 4
SCALE_ROWS = 8


def swap_tables(rows, cols):
    def table(partner):
        pairs = []
        for r in range(rows):
            for c in range(cols):
                r2, c2 = partner(r, c)
                pairs.append((r * cols + c, r2 * cols + c2))
        return pairs

    idle = 2 if cols % 4 == 0 else 1

    def across_rows(r, c):
        other = r + 1 if r % 2 else r - 1
        return (other, c) if 0 <= other < rows else (r, c ^ idle)

    def across_cols(r, c):
        other = c + 1 if c % 2 else c - 1
        return (r, other) if 0 <= other < cols else (r ^ 1, c)

    return [
        table(across_cols),
        table(lambda r, c: (r, c ^ 1)),
        table(across_rows),
        table(lambda r, c: (r ^ 1, c)),
    ]


def faces_of_partners():
    odd_row = lax.rem(lax.axis_index("row"), 2)
    odd_col = lax.rem(lax.axis_index("col"), 2)
    return [2 + odd_col, 3 - odd_col, odd_row, 1 - odd_row]


def face_slice(face, depth):
    return pl.ds(pl.multiple_of(face * depth, depth), depth)


def face_sign(face):
    return (2 * lax.rem(face, 2) - 1).astype(jnp.float32)


def masked(value, count):
    unknown = lax.broadcasted_iota(jnp.int32, value.shape, 0)
    return jnp.where(unknown < count, value, 0.0)


def column_sum(value):
    return jnp.sum(value, axis=0, keepdims=True)


def gap_kernel(gap_hbm, rows_hbm, modes_hbm, coarse_hbm, *refs):
    out_refs, (counts_ref, modes_ref, coarse_ref, gap, field, rows, sems) = refs[:PARTNERS], refs[PARTNERS:]
    moves = [(gap_hbm, gap), (rows_hbm, rows), (modes_hbm, modes_ref), (coarse_hbm, coarse_ref)]
    copies = [pltpu.make_async_copy(source, target, sems.at[at]) for at, (source, target) in enumerate(moves)]
    for copy in copies:
        copy.start()
    copies[0].wait()
    depth = gap.shape[2]
    faces = faces_of_partners()
    for face in range(PARTNERS):
        sign = 1.0 if face % 2 else -1.0
        block = gap[:, face, :].astype(jnp.float32) * sign
        field[face * depth : (face + 1) * depth, :] = block.T
    for face, out_ref in zip(faces, out_refs):
        out_ref[...] = field[face_slice(face, depth), :]
    copies[1].wait()
    for partner, face in enumerate(faces):
        counts_ref[partner : partner + 1, :] = jnp.full((1, counts_ref.shape[1]), rows[0, 0, face], jnp.int32)
    copies[2].wait()
    copies[3].wait()


def high_low(value):
    high = value.astype(jnp.bfloat16)
    return high, (value - high.astype(jnp.float32)).astype(jnp.bfloat16)


def turn_kernel(operator_hbm, modes_ref, coarse_ref, operator_ref, turned_ref, parts_ref, sem):
    copy = pltpu.make_async_copy(operator_hbm, operator_ref, sem)
    copy.start()
    turned_ref[...] = modes_ref[...].astype(jnp.float32).T.astype(jnp.bfloat16)
    unknowns = coarse_ref.shape[1]
    high, low = high_low(coarse_ref[...])
    parts_ref[:, :unknowns] = high
    parts_ref[:, unknowns : 2 * unknowns] = high
    parts_ref[:, 2 * unknowns :] = low
    copy.wait()


def columns_kernel(*refs):
    field_refs, out_ref = refs[:PARTNERS], refs[PARTNERS]
    for face, ref in zip(faces_of_partners(), field_refs):
        out_ref[face] = ref[...].T


def read_pair(mine_ref, got_ref, count, scaled):
    depth = mine_ref.shape[0] - (SCALE_ROWS if scaled else 0)
    return mine_ref[:depth, :], got_ref[:depth, :]


def scale_of(ref):
    depth = ref.shape[0] - SCALE_ROWS
    return ref[depth : depth + 1, :]


def widest(own_scale, got_refs, counts):
    top = own_scale
    for ref, count in zip(got_refs, counts):
        top = jnp.maximum(top, jnp.where(count > 0, scale_of(ref), own_scale))
    return top


def glued(mine_refs, got_refs, counts, scaled):
    fields = []
    if scaled:
        own_scale = scale_of(mine_refs[0])
        top = widest(own_scale, got_refs, counts)
        own_factor = own_scale / top
    else:
        top = None
    for mine_ref, got_ref, count in zip(mine_refs, got_refs, counts):
        mine, got = read_pair(mine_ref, got_ref, count, scaled)
        if scaled:
            mine, got = mine * own_factor, got * (scale_of(got_ref) / top)
        fields.append(masked(mine + got, count))
    return fields, top


def counts_of(counts_ref):
    return [counts_ref[partner : partner + 1, :] for partner in range(PARTNERS)]


def coeffs_kernel(scaled, counts_ref, modes_ref, *refs):
    mine_refs, got_refs, out_ref, flat = refs[:4], refs[4:8], refs[8], refs[9]
    faces = faces_of_partners()
    fields, top = glued(mine_refs, got_refs, counts_of(counts_ref), scaled)
    depth = fields[0].shape[0]
    for face, field in zip(faces, fields):
        flat[face_slice(face, depth), :] = field.astype(jnp.bfloat16)
    count = modes_ref.shape[0]
    out_ref[:count, :] = jnp.dot(modes_ref[...], flat[...], preferred_element_type=jnp.float32)
    if scaled:
        out_ref[count:, :] = jnp.broadcast_to(top, (SCALE_ROWS, top.shape[1]))


def coarse_kernel(cols, scaled, parts_ref, turned_ref, *refs):
    block_refs, out_refs, stack = refs[:cols], refs[cols:-1], refs[-1]
    mine = lax.axis_index("col")
    count = parts_ref.shape[0]
    unknowns = cols * count
    depth = turned_ref.shape[0] // PARTNERS
    top = None
    if scaled:
        top = functools.reduce(jnp.maximum, [scale_of(ref) for ref in block_refs])
    for step, ref in enumerate(block_refs):
        block = ref[:count, :]
        if scaled:
            block = block * (scale_of(ref) / top)
        high, low = high_low(block)
        start = (mine ^ step) * count
        for base, part in ((0, high), (unknowns, low), (2 * unknowns, high)):
            stack[pl.ds(pl.multiple_of(base + start, count), count), :] = part
    coarse = jnp.dot(parts_ref[...], stack[...], preferred_element_type=jnp.float32).astype(jnp.bfloat16)
    for face, out_ref in zip(faces_of_partners(), out_refs):
        out_ref[:depth, :] = jnp.dot(turned_ref[face_slice(face, depth), :], coarse, preferred_element_type=jnp.float32)
        if scaled:
            out_ref[depth:, :] = jnp.broadcast_to(top, (SCALE_ROWS, top.shape[1]))


def apply_dual(operator_ref, fields, faces, flat):
    depth = fields[0].shape[0]
    for face, field in zip(faces, fields):
        flat[face_slice(face, depth), :] = (field * face_sign(face)).astype(jnp.bfloat16)
    signed = flat[...]
    return [
        jnp.dot(operator_ref[face_slice(face, depth), :], signed, preferred_element_type=jnp.float32) * face_sign(face)
        for face in faces
    ]


def apply_dual_whole(operator_ref, fields, faces, flat, image):
    depth = fields[0].shape[0]
    for face, field in zip(faces, fields):
        flat[face_slice(face, depth), :] = (field * face_sign(face)).astype(jnp.bfloat16)
    image[...] = jnp.dot(operator_ref[...], flat[...], preferred_element_type=jnp.float32)
    return [image[face_slice(face, depth), :] * face_sign(face) for face in faces]


def first_kernel(counts_ref, operator_ref, *refs):
    mine_refs, got_refs, part_refs, got_part_refs = refs[:4], refs[4:8], refs[8:12], refs[12:16]
    vector_refs, image_refs, sums_ref, flat = refs[16:20], refs[20:24], refs[24], refs[25]
    faces = faces_of_partners()
    counts = counts_of(counts_ref)
    residuals, _ = glued(mine_refs, got_refs, counts, False)
    parts, _ = glued(part_refs, got_part_refs, counts, False)
    fields = [residual - part for residual, part in zip(residuals, parts)]
    for ref, field in zip(vector_refs, fields):
        ref[...] = field
    images = apply_dual(operator_ref, fields, faces, flat)
    largest = functools.reduce(jnp.maximum, [jnp.max(jnp.abs(value), axis=0, keepdims=True) for value in images])
    largest = jnp.where(largest > 0.0, largest, 1.0)
    inverse = 1.0 / largest
    depth = fields[0].shape[0]
    norm, curvature = 0.0, 0.0
    for ref, field, value in zip(image_refs, fields, images):
        norm += column_sum(field * field)
        curvature += column_sum(field * value)
        ref[:depth, :] = value * inverse
        ref[depth:, :] = jnp.broadcast_to(largest, (SCALE_ROWS, largest.shape[1]))
    sums_ref[0:1, :] = 0.5 * norm
    sums_ref[1:2, :] = curvature


def second_kernel(counts_ref, operator_ref, sums_in_ref, *refs):
    mine_refs, got_refs, part_refs, got_part_refs, first_refs = (refs[4 * i : 4 * i + 4] for i in range(5))
    vector_refs, sums_ref, flat, image = refs[21:25], refs[25], refs[26], refs[27]
    faces = faces_of_partners()
    counts = counts_of(counts_ref)
    images, image_scale = glued(mine_refs, got_refs, counts, True)
    parts, part_scale = glued(part_refs, got_part_refs, counts, True)
    top = jnp.maximum(image_scale, part_scale)
    fields = [value * (image_scale / top) - part * (part_scale / top) for value, part in zip(images, parts)]
    for ref, field in zip(vector_refs, fields):
        ref[...] = field
    own_scale = scale_of(mine_refs[0])
    depth = fields[0].shape[0]
    second_images = apply_dual_whole(operator_ref, fields, faces, flat, image)
    mixed, square, cross, bend = 0.0, 0.0, 0.0, 0.0
    reach = 0.0
    for first_ref, mine_ref, field, value in zip(first_refs, mine_refs, fields, second_images):
        first = first_ref[...]
        mixed += column_sum(first * field)
        square += column_sum(field * field)
        cross += column_sum(first * value)
        reach += column_sum(field * mine_ref[:depth, :])
        bend += column_sum(field * value)
    rows = [sums_in_ref[0:1, :], sums_in_ref[1:2, :], 0.5 * mixed, 0.5 * square, cross + own_scale * reach, bend, top, top]
    table = jnp.concatenate(rows, axis=0)
    sums_ref[...] = jnp.broadcast_to(table[None], sums_ref.shape)


def last_kernel(sums_ref, first_ref, *refs):
    second_refs, (out_hbm, turned, out, sems) = refs[:PARTNERS], refs[PARTNERS:]
    device = lax.axis_index("row") * lax.axis_size("col") + lax.axis_index("col")
    every = sums_ref[...]
    scales = every[:, 6:7, :]
    top = jnp.max(scales, axis=0, keepdims=True)
    share = scales / top
    norm = jnp.sum(every[:, 0:1, :], axis=0)
    curvature = jnp.sum(every[:, 1:2, :], axis=0)
    mixed = jnp.sum(every[:, 2:3, :] * share, axis=0)
    square = jnp.sum(every[:, 3:4, :] * share * share, axis=0)
    cross = jnp.sum(every[:, 4:5, :] * share, axis=0)
    bend = jnp.sum(every[:, 5:6, :] * share * share, axis=0)
    step = norm / curvature
    reach = step * top[0]
    fresh = norm - 2.0 * reach * mixed + reach * (reach * square)
    ratio = fresh / norm
    grow = 1.0 + ratio
    next_curvature = grow * (grow * curvature) - grow * (reach * cross) + reach * (reach * bend)
    next_step = fresh / next_curvature
    along_first = step + next_step * grow
    along_second = next_step * (step * sums_ref[device, 6:7, :])
    columns = first_ref.shape[1]
    rows = jnp.concatenate([along_first, along_second] + [along_first] * 6, axis=0).T
    for face, ref in zip(faces_of_partners(), second_refs):
        turned[face] = ref[...].T
    copies = []
    pieces = 2
    for piece in range(pieces):
        part = slice(piece * columns // pieces, (piece + 1) * columns // pieces)
        for face in range(PARTNERS):
            out[part, face, :] = rows[part, 0:1] * first_ref[face, part, :] - rows[part, 1:2] * turned[face, part, :]
        copies.append(pltpu.make_async_copy(out.at[part], out_hbm.at[part], sems.at[piece]))
        copies[-1].start()
    for copy in copies:
        copy.wait()


VMEM = pl.BlockSpec(memory_space=pltpu.VMEM)
HBM = pl.BlockSpec(memory_space=pltpu.HBM)
ANY = pl.BlockSpec(memory_space=pl.ANY)


def run(kernel, name, outs, scratch, in_specs, args, flops=0, out_spec=VMEM):
    moved = sum(a.size * a.dtype.itemsize for a in args)
    return pl.pallas_call(
        kernel,
        name=name,
        out_shape=outs,
        in_specs=in_specs,
        out_specs=jax.tree.map(lambda _: out_spec, outs),
        scratch_shapes=scratch,
        compiler_params=pltpu.CompilerParams(vmem_limit_bytes=16 * 2**20),
        cost_estimate=pl.CostEstimate(flops=flops, bytes_accessed=moved, transcendentals=0),
    )(*args)


def on_device(rows, cols, local_gap, dual_ops, geneo_modes, coarse_inverse, face_rows):
    tables = swap_tables(rows, cols)
    gap = local_gap[0, 0]
    operator = dual_ops[0, 0]
    modes = geneo_modes[0, 0]
    coarse_block = coarse_inverse[0]
    columns, _, depth = gap.shape
    unknowns = operator.shape[0]
    count = modes.shape[0]

    def shape(*dims, dtype=jnp.float32):
        return jax.ShapeDtypeStruct(dims, dtype)

    def swap(fields):
        return [lax.ppermute(field, ("row", "col"), pairs) for field, pairs in zip(fields, tables)]

    def gather(block):
        steps = [[(c, c ^ step) for c in range(cols)] for step in range(1, cols)]
        return [block] + [lax.ppermute(block, "col", pairs) for pairs in steps]

    def four(height):
        return [shape(height, columns)] * PARTNERS

    flat = pltpu.VMEM((unknowns, columns), jnp.bfloat16)
    wide = pltpu.VMEM((unknowns, columns), jnp.float32)
    tall = depth + SCALE_ROWS

    def in_hbm(array):
        return pltpu.with_memory_space_constraint(array, pltpu.HBM)

    *gaps, counts, modes, coarse_block = run(
        gap_kernel, "gap",
        four(depth)
        + [
            shape(PARTNERS, columns, dtype=jnp.int32),
            shape(*modes.shape, dtype=modes.dtype),
            shape(*coarse_block.shape),
        ],
        [pltpu.VMEM(gap.shape, gap.dtype), wide, pltpu.SMEM(face_rows.shape, jnp.int32), pltpu.SemaphoreType.DMA((4,))],
        [HBM] * 4, list(map(in_hbm, (gap, face_rows, modes, coarse_block))),
    )
    got_gaps = swap(gaps)
    coeffs = run(
        functools.partial(coeffs_kernel, False), "coeffs", shape(count, columns), [flat],
        [VMEM] * 10, [counts, modes, *gaps, *got_gaps],
    )
    blocks = gather(coeffs)
    operator, turned, coarse_parts = run(
        turn_kernel, "turn",
        [
            shape(*operator.shape, dtype=operator.dtype),
            shape(unknowns, count, dtype=modes.dtype),
            shape(count, 3 * cols * count, dtype=jnp.bfloat16),
        ],
        [pltpu.SemaphoreType.DMA], [HBM, VMEM, VMEM], [in_hbm(operator), modes, coarse_block],
    )
    stack = pltpu.VMEM((3 * cols * count, columns), jnp.bfloat16)
    parts = run(
        functools.partial(coarse_kernel, cols, False), "coarse", four(depth), [stack],
        [VMEM] * (2 + cols), [coarse_parts, turned, *blocks],
    )
    got_parts = swap(parts)
    *first, sums = run(
        first_kernel, "first", four(depth) + four(tall) + [shape(2, columns)], [flat],
        [VMEM] * 18, [counts, operator, *gaps, *got_gaps, *parts, *got_parts],
    )
    first, images = first[:PARTNERS], first[PARTNERS:]
    got_images = swap(images)
    coeffs = run(
        functools.partial(coeffs_kernel, True), "coeffs2", shape(count + SCALE_ROWS, columns), [flat],
        [VMEM] * 10, [counts, modes, *images, *got_images],
    )
    parts = run(
        functools.partial(coarse_kernel, cols, True), "coarse2", four(tall), [stack],
        [VMEM] * (2 + cols), [coarse_parts, turned, *gather(coeffs)],
    )
    got_parts = swap(parts)
    first_turned = run(
        columns_kernel, "columns", shape(PARTNERS, columns, depth), [], [VMEM] * 4, first,
    )
    *second, sums = run(
        second_kernel, "second", four(depth) + [shape(rows * cols, 8, columns)], [flat, wide],
        [VMEM] * 23 + [ANY], [counts, operator, sums, *images, *got_images, *parts, *got_parts, *first, first_turned],
    )
    every = lax.all_to_all(sums, ("row", "col"), 0, 0)
    whole = (columns, PARTNERS, depth)
    out = run(
        last_kernel, "last", shape(*whole),
        [pltpu.VMEM((PARTNERS, columns, depth), jnp.float32), pltpu.VMEM(whole, jnp.float32), pltpu.SemaphoreType.DMA((2,))],
        [VMEM] * 6, [every, first_turned, *second], out_spec=HBM,
    )
    return out[None, None]


def solution(mesh):
    rows, cols = mesh.shape["row"], mesh.shape["col"]

    def body(*arrays):
        return on_device(rows, cols, *arrays)

    return jax.shard_map(
        body,
        mesh=mesh,
        in_specs=(
            P("row", "col", None, None, None),
            P("row", "col", None, None),
            P("row", "col", None, None),
            P("row", "col", None),
            P("row", "col", None),
        ),
        out_specs=P("row", "col", None, None, None),
        check_vma=False,
    )
```

```python
import functools

import jax
import jax.numpy as jnp
from jax import lax
from jax.experimental import pallas as pl
from jax.experimental.pallas import tpu as pltpu
from jax.sharding import PartitionSpec as P

PARTNERS = 4
SCALE_ROWS = 8


def swap_tables(rows, cols):
    def table(partner):
        pairs = []
        for r in range(rows):
            for c in range(cols):
                r2, c2 = partner(r, c)
                pairs.append((r * cols + c, r2 * cols + c2))
        return pairs

    idle = 2 if cols % 4 == 0 else 1

    def across_rows(r, c):
        other = r + 1 if r % 2 else r - 1
        return (other, c) if 0 <= other < rows else (r, c ^ idle)

    def across_cols(r, c):
        other = c + 1 if c % 2 else c - 1
        return (r, other) if 0 <= other < cols else (r ^ 1, c)

    return [
        table(across_cols),
        table(lambda r, c: (r, c ^ 1)),
        table(across_rows),
        table(lambda r, c: (r ^ 1, c)),
    ]


def faces_of_partners():
    odd_row = lax.rem(lax.axis_index("row"), 2)
    odd_col = lax.rem(lax.axis_index("col"), 2)
    return [2 + odd_col, 3 - odd_col, odd_row, 1 - odd_row]


def face_slice(face, depth):
    return pl.ds(pl.multiple_of(face * depth, depth), depth)


def face_sign(face):
    return (2 * lax.rem(face, 2) - 1).astype(jnp.float32)


def masked(value, count):
    unknown = lax.broadcasted_iota(jnp.int32, value.shape, 0)
    return jnp.where(unknown < count, value, 0.0)


def column_sum(value):
    return jnp.sum(value, axis=0, keepdims=True)


def gap_kernel(gap_hbm, *refs):
    out_refs, (gap, field, sem) = refs[:PARTNERS], refs[PARTNERS:]
    copy = pltpu.make_async_copy(gap_hbm, gap, sem)
    copy.start()
    copy.wait()
    depth = gap.shape[2]
    for face in range(PARTNERS):
        sign = 1.0 if face % 2 else -1.0
        block = gap[:, face, :].astype(jnp.float32) * sign
        field[face * depth : (face + 1) * depth, :] = block.T
    for face, out_ref in zip(faces_of_partners(), out_refs):
        out_ref[...] = field[face_slice(face, depth), :]


def high_low(value):
    high = value.astype(jnp.bfloat16)
    return high, (value - high.astype(jnp.float32)).astype(jnp.bfloat16)


def prepare_kernel(rows_hbm, modes_hbm, coarse_hbm, operator_hbm, after_ref, *refs):
    del after_ref
    counts_ref, modes_ref, operator_ref, turned_ref, parts_ref, rows, coarse, sems = refs
    moves = [(modes_hbm, modes_ref), (coarse_hbm, coarse), (rows_hbm, rows), (operator_hbm, operator_ref)]
    copies = [pltpu.make_async_copy(source, target, sems.at[at]) for at, (source, target) in enumerate(moves)]
    for copy in copies:
        copy.start()
    copies[0].wait()
    turned_ref[...] = modes_ref[...].astype(jnp.float32).T.astype(jnp.bfloat16)
    copies[1].wait()
    unknowns = coarse.shape[1]
    high, low = high_low(coarse[...])
    parts_ref[:, :unknowns] = high
    parts_ref[:, unknowns : 2 * unknowns] = high
    parts_ref[:, 2 * unknowns :] = low
    copies[2].wait()
    for partner, face in enumerate(faces_of_partners()):
        counts_ref[partner : partner + 1, :] = jnp.full((1, counts_ref.shape[1]), rows[0, 0, face], jnp.int32)
    copies[3].wait()


def columns_kernel(*refs):
    field_refs, out_ref = refs[:PARTNERS], refs[PARTNERS]
    for face, ref in zip(faces_of_partners(), field_refs):
        out_ref[face] = ref[...].T


def scale_of(ref):
    depth = ref.shape[0] - SCALE_ROWS
    return ref[depth : depth + 1, :]


def set_scale(ref, scale):
    depth = ref.shape[0] - SCALE_ROWS
    ref[depth:, :] = jnp.broadcast_to(scale, (SCALE_ROWS, scale.shape[1]))


def widest(own_scale, got_refs, counts):
    top = own_scale
    for ref, count in zip(got_refs, counts):
        top = jnp.maximum(top, jnp.where(count > 0, scale_of(ref), own_scale))
    return top


def counts_of(counts_ref):
    return [counts_ref[partner : partner + 1, :] for partner in range(PARTNERS)]


def sum_of_pair(mine_ref, got_ref, depth, top):
    mine, got = mine_ref[:depth, :], got_ref[:depth, :]
    if top is not None:
        mine, got = mine * (scale_of(mine_ref) / top), got * (scale_of(got_ref) / top)
    return mine + got


def coeffs_kernel(scaled, counts_ref, modes_ref, *refs):
    mine_refs, got_refs, out_ref, flat = refs[:4], refs[4:8], refs[8], refs[9]
    counts = counts_of(counts_ref)
    depth = flat.shape[0] // PARTNERS
    top = widest(scale_of(mine_refs[0]), got_refs, counts) if scaled else None
    for face, mine_ref, got_ref, count in zip(faces_of_partners(), mine_refs, got_refs, counts):
        field = masked(sum_of_pair(mine_ref, got_ref, depth, top), count)
        flat[face_slice(face, depth), :] = field.astype(jnp.bfloat16)
    modes = modes_ref.shape[0]
    out_ref[:modes, :] = jnp.dot(modes_ref[...], flat[...], preferred_element_type=jnp.float32)
    if scaled:
        set_scale(out_ref, top)


def base_kernel(scaled, counts_ref, *refs):
    mine_refs, got_refs, part_refs, out_refs = (refs[4 * i : 4 * i + 4] for i in range(4))
    top = scale_of(part_refs[0]) if scaled else None
    depth = mine_refs[0].shape[0] - (SCALE_ROWS if scaled else 0)
    for mine_ref, got_ref, part_ref, out_ref, count in zip(mine_refs, got_refs, part_refs, out_refs, counts_of(counts_ref)):
        out_ref[:depth, :] = masked(sum_of_pair(mine_ref, got_ref, depth, top) - part_ref[:depth, :], count)
        if scaled:
            set_scale(out_ref, top)


def coarse_kernel(cols, scaled, parts_ref, turned_ref, *refs):
    block_refs, out_refs, stack = refs[:cols], refs[cols:-1], refs[-1]
    mine = lax.axis_index("col")
    count = parts_ref.shape[0]
    unknowns = cols * count
    depth = turned_ref.shape[0] // PARTNERS
    top = None
    if scaled:
        top = functools.reduce(jnp.maximum, [scale_of(ref) for ref in block_refs])
    for step, ref in enumerate(block_refs):
        block = ref[:count, :]
        if scaled:
            block = block * (scale_of(ref) / top)
        high, low = high_low(block)
        start = (mine ^ step) * count
        for base, part in ((0, high), (unknowns, low), (2 * unknowns, high)):
            stack[pl.ds(pl.multiple_of(base + start, count), count), :] = part
    coarse = jnp.dot(parts_ref[...], stack[...], preferred_element_type=jnp.float32).astype(jnp.bfloat16)
    for face, out_ref in zip(faces_of_partners(), out_refs):
        out_ref[:depth, :] = jnp.dot(turned_ref[face_slice(face, depth), :], coarse, preferred_element_type=jnp.float32)
        if scaled:
            out_ref[depth:, :] = jnp.broadcast_to(top, (SCALE_ROWS, top.shape[1]))


def dual_rows(operator_ref, flat, face):
    depth = flat.shape[0] // PARTNERS
    return jnp.dot(operator_ref[face_slice(face, depth), :], flat[...], preferred_element_type=jnp.float32) * face_sign(face)


def first_kernel(counts_ref, operator_ref, *refs):
    base_refs, got_part_refs, vector_refs, image_refs = (refs[4 * i : 4 * i + 4] for i in range(4))
    sums_ref, flat = refs[16:]
    faces = faces_of_partners()
    depth = flat.shape[0] // PARTNERS
    norm, curvature, largest = 0.0, 0.0, 0.0
    for face, base_ref, got_ref, vector_ref, count in zip(faces, base_refs, got_part_refs, vector_refs, counts_of(counts_ref)):
        field = base_ref[...] - masked(got_ref[...], count)
        vector_ref[...] = field
        flat[face_slice(face, depth), :] = (field * face_sign(face)).astype(jnp.bfloat16)
        norm += column_sum(field * field)
    for face, vector_ref, image_ref in zip(faces, vector_refs, image_refs):
        value = dual_rows(operator_ref, flat, face)
        image_ref[:depth, :] = value
        curvature += column_sum(vector_ref[...] * value)
        largest = jnp.maximum(largest, jnp.max(jnp.abs(value), axis=0, keepdims=True))
    largest = jnp.where(largest > 0.0, largest, 1.0)
    inverse = 1.0 / largest
    for image_ref in image_refs:
        image_ref[:depth, :] = image_ref[:depth, :] * inverse
        set_scale(image_ref, largest)
    sums_ref[0:1, :] = 0.5 * norm
    sums_ref[1:2, :] = curvature


def second_kernel(counts_ref, operator_ref, sums_in_ref, *refs):
    base_refs, got_part_refs, image_refs, first_refs = (refs[4 * i : 4 * i + 4] for i in range(4))
    after_ref, turned_ref, sums_ref, flat = refs[16:20]
    vector_refs = refs[20:]
    del after_ref
    faces = faces_of_partners()
    counts = counts_of(counts_ref)
    depth = flat.shape[0] // PARTNERS
    own_scale = scale_of(base_refs[0])
    top = widest(own_scale, got_part_refs, counts)
    own_factor = own_scale / top
    mixed, square, reach, bend = 0.0, 0.0, 0.0, 0.0
    for face, base_ref, got_ref, vector_ref, count in zip(faces, base_refs, got_part_refs, vector_refs, counts):
        field = base_ref[:depth, :] * own_factor - masked(got_ref[:depth, :] * (scale_of(got_ref) / top), count)
        vector_ref[...] = field
        flat[face_slice(face, depth), :] = (field * face_sign(face)).astype(jnp.bfloat16)
    for face, vector_ref, first_ref, image_ref in zip(faces, vector_refs, first_refs, image_refs):
        value = dual_rows(operator_ref, flat, face)
        field = vector_ref[...]
        mixed += column_sum(first_ref[...] * field)
        square += column_sum(field * field)
        reach += column_sum(field * image_ref[:depth, :])
        bend += column_sum(field * value)
        turned_ref[face] = field.T
    cross = (2.0 * scale_of(image_refs[0])) * reach
    rows = [sums_in_ref[0:1, :], sums_in_ref[1:2, :], 0.5 * mixed, 0.5 * square, cross, bend, top, top]
    table = jnp.concatenate(rows, axis=0)
    sums_ref[...] = jnp.broadcast_to(table[None], sums_ref.shape)


def last_kernel(sums_ref, first_ref, second_ref, out_hbm, out, sems):
    device = lax.axis_index("col") * lax.axis_size("row") + lax.axis_index("row")
    every = sums_ref[...]
    scales = every[:, 6:7, :]
    top = jnp.max(scales, axis=0, keepdims=True)
    share = scales / top
    norm = jnp.sum(every[:, 0:1, :], axis=0)
    curvature = jnp.sum(every[:, 1:2, :], axis=0)
    mixed = jnp.sum(every[:, 2:3, :] * share, axis=0)
    square = jnp.sum(every[:, 3:4, :] * share * share, axis=0)
    cross = jnp.sum(every[:, 4:5, :] * share, axis=0)
    bend = jnp.sum(every[:, 5:6, :] * share * share, axis=0)
    step = norm / curvature
    reach = step * top[0]
    fresh = norm - 2.0 * reach * mixed + reach * (reach * square)
    ratio = fresh / norm
    grow = 1.0 + ratio
    next_curvature = grow * (grow * curvature) - grow * (reach * cross) + reach * (reach * bend)
    next_step = fresh / next_curvature
    along_first = step + next_step * grow
    along_second = next_step * (step * sums_ref[device, 6:7, :])
    columns = first_ref.shape[1]
    rows = jnp.concatenate([along_first, along_second] + [along_first] * 6, axis=0).T
    copies = []
    pieces = 2
    for piece in range(pieces):
        part = slice(piece * columns // pieces, (piece + 1) * columns // pieces)
        for face in range(PARTNERS):
            out[part, face, :] = rows[part, 0:1] * first_ref[face, part, :] - rows[part, 1:2] * second_ref[face, part, :]
        copies.append(pltpu.make_async_copy(out.at[part], out_hbm.at[part], sems.at[piece]))
        copies[-1].start()
    for copy in copies:
        copy.wait()


VMEM = pl.BlockSpec(memory_space=pltpu.VMEM)
HBM = pl.BlockSpec(memory_space=pltpu.HBM)
ANY = pl.BlockSpec(memory_space=pl.ANY)


def run(kernel, name, outs, scratch, in_specs, args, flops=0, out_spec=VMEM):
    moved = sum(a.size * a.dtype.itemsize for a in args)
    return pl.pallas_call(
        kernel,
        name=name,
        out_shape=outs,
        in_specs=in_specs,
        out_specs=jax.tree.map(lambda _: out_spec, outs),
        scratch_shapes=scratch,
        compiler_params=pltpu.CompilerParams(vmem_limit_bytes=16 * 2**20),
        cost_estimate=pl.CostEstimate(flops=flops, bytes_accessed=moved, transcendentals=0),
    )(*args)


def on_device(rows, cols, local_gap, dual_ops, geneo_modes, coarse_inverse, face_rows):
    tables = swap_tables(rows, cols)
    gap = local_gap[0, 0]
    operator = dual_ops[0, 0]
    modes = geneo_modes[0, 0]
    coarse_block = coarse_inverse[0]
    columns, _, depth = gap.shape
    unknowns = operator.shape[0]
    count = modes.shape[0]

    def shape(*dims, dtype=jnp.float32):
        return jax.ShapeDtypeStruct(dims, dtype)

    def swap(fields):
        return [lax.ppermute(field, ("row", "col"), pairs) for field, pairs in zip(fields, tables)]

    def gather(block):
        steps = [[(c, c ^ step) for c in range(cols)] for step in range(1, cols)]
        return [block] + [lax.ppermute(block, "col", pairs) for pairs in steps]

    def four(height):
        return [shape(height, columns)] * PARTNERS

    flat = pltpu.VMEM((unknowns, columns), jnp.bfloat16)
    wide = pltpu.VMEM((unknowns, columns), jnp.float32)
    tall = depth + SCALE_ROWS

    def in_hbm(array):
        return pltpu.with_memory_space_constraint(array, pltpu.HBM)

    gaps = run(
        gap_kernel, "gap", four(depth), [pltpu.VMEM(gap.shape, gap.dtype), wide, pltpu.SemaphoreType.DMA],
        [HBM], [in_hbm(gap)],
    )
    got_gaps = swap(gaps)
    counts, modes, operator, turned, coarse_parts = run(
        prepare_kernel, "prepare",
        [
            shape(PARTNERS, columns, dtype=jnp.int32),
            shape(*modes.shape, dtype=modes.dtype),
            shape(*operator.shape, dtype=operator.dtype),
            shape(unknowns, count, dtype=modes.dtype),
            shape(count, 3 * cols * count, dtype=jnp.bfloat16),
        ],
        [
            pltpu.SMEM(face_rows.shape, jnp.int32),
            pltpu.VMEM(coarse_block.shape, jnp.float32),
            pltpu.SemaphoreType.DMA((4,)),
        ],
        [HBM] * 4 + [ANY], [*map(in_hbm, (face_rows, modes, coarse_block, operator)), gaps[PARTNERS - 1]],
    )
    stack = pltpu.VMEM((3 * cols * count, columns), jnp.bfloat16)

    def correction(scaled, fields, got_fields):
        extra = SCALE_ROWS if scaled else 0
        name = "second" if scaled else "first"
        coeffs = run(
            functools.partial(coeffs_kernel, scaled), name + "_coeffs", shape(count + extra, columns), [flat],
            [VMEM] * 10, [counts, modes, *fields, *got_fields],
        )
        parts = run(
            functools.partial(coarse_kernel, cols, scaled), name + "_coarse", four(depth + extra), [stack],
            [VMEM] * (2 + cols), [coarse_parts, turned, *gather(coeffs)],
        )
        got_parts = swap(parts)
        base = run(
            functools.partial(base_kernel, scaled), name + "_base", four(depth + extra), [],
            [VMEM] * 13, [counts, *fields, *got_fields, *parts],
        )
        return base, got_parts

    base, got_parts = correction(False, gaps, got_gaps)
    *first, sums = run(
        first_kernel, "first", four(depth) + four(tall) + [shape(2, columns)], [flat],
        [VMEM] * 10, [counts, operator, *base, *got_parts],
    )
    first, images = first[:PARTNERS], first[PARTNERS:]
    got_images = swap(images)
    first_turned = run(columns_kernel, "columns", shape(PARTNERS, columns, depth), [], [VMEM] * 4, first)
    base, got_parts = correction(True, images, got_images)
    second_turned, sums = run(
        second_kernel, "second", [shape(PARTNERS, columns, depth), shape(rows * cols, 8, columns)],
        [flat] + [pltpu.VMEM((depth, columns), jnp.float32)] * PARTNERS,
        [VMEM] * 19 + [ANY], [counts, operator, sums, *base, *got_parts, *images, *first, first_turned],
    )
    every = lax.all_to_all(sums, ("col", "row"), 0, 0)
    whole = (columns, PARTNERS, depth)
    out = run(
        last_kernel, "last", shape(*whole),
        [pltpu.VMEM(whole, jnp.float32), pltpu.SemaphoreType.DMA((2,))],
        [VMEM] * 3, [every, first_turned, second_turned], out_spec=HBM,
    )
    return out[None, None]


def solution(mesh):
    rows, cols = mesh.shape["row"], mesh.shape["col"]

    def body(*arrays):
        return on_device(rows, cols, *arrays)

    return jax.shard_map(
        body,
        mesh=mesh,
        in_specs=(
            P("row", "col", None, None, None),
            P("row", "col", None, None),
            P("row", "col", None, None),
            P("row", "col", None),
            P("row", "col", None),
        ),
        out_specs=P("row", "col", None, None, None),
        check_vma=False,
    )
```

```python
import functools

import jax
import jax.numpy as jnp
from jax import lax
from jax.experimental import pallas as pl
from jax.experimental.pallas import tpu as pltpu
from jax.sharding import PartitionSpec as P

PARTNERS = 4
SCALE_ROWS = 8


def swap_tables(rows, cols):
    def table(partner):
        pairs = []
        for r in range(rows):
            for c in range(cols):
                r2, c2 = partner(r, c)
                pairs.append((r * cols + c, r2 * cols + c2))
        return pairs

    def idle(c):
        return c - c % 4 + (1, 3, 0, 2)[c % 4] if cols % 4 == 0 else c ^ 1

    def across_rows(r, c):
        other = r + 1 if r % 2 else r - 1
        return (other, c) if 0 <= other < rows else (r, idle(c))

    def across_cols(r, c):
        other = c + 1 if c % 2 else c - 1
        return (r, other) if 0 <= other < cols else (r ^ 1, c)

    return [
        table(across_cols),
        table(lambda r, c: (r, c ^ 1)),
        table(across_rows),
        table(lambda r, c: (r ^ 1, c)),
    ]


def faces_of_partners():
    odd_row = lax.rem(lax.axis_index("row"), 2)
    odd_col = lax.rem(lax.axis_index("col"), 2)
    return [2 + odd_col, 3 - odd_col, odd_row, 1 - odd_row]


def face_slice(face, depth):
    return pl.ds(pl.multiple_of(face * depth, depth), depth)


def face_sign(face):
    return (2 * lax.rem(face, 2) - 1).astype(jnp.float32)


def masked(value, count):
    unknown = lax.broadcasted_iota(jnp.int32, value.shape, 0)
    return jnp.where(unknown < count, value, 0.0)


def column_sum(value):
    return jnp.sum(value, axis=0, keepdims=True)


def gap_kernel(gap_hbm, *refs):
    out_refs, (gap, field, sem) = refs[:PARTNERS], refs[PARTNERS:]
    copy = pltpu.make_async_copy(gap_hbm, gap, sem)
    copy.start()
    copy.wait()
    depth = gap.shape[2]
    for face in range(PARTNERS):
        sign = 1.0 if face % 2 else -1.0
        block = gap[:, face, :].astype(jnp.float32) * sign
        field[face * depth : (face + 1) * depth, :] = block.T
    for face, out_ref in zip(faces_of_partners(), out_refs):
        out_ref[...] = field[face_slice(face, depth), :]


def high_low(value):
    high = value.astype(jnp.bfloat16)
    return high, (value - high.astype(jnp.float32)).astype(jnp.bfloat16)


def prepare_kernel(rows_hbm, modes_hbm, coarse_hbm, operator_hbm, after_ref, *refs):
    del after_ref
    counts_ref, modes_ref, operator_ref, turned_ref, parts_ref, rows, coarse, sems = refs
    moves = [(modes_hbm, modes_ref), (coarse_hbm, coarse), (rows_hbm, rows), (operator_hbm, operator_ref)]
    copies = [pltpu.make_async_copy(source, target, sems.at[at]) for at, (source, target) in enumerate(moves)]
    for copy in copies:
        copy.start()
    copies[0].wait()
    turned_ref[...] = modes_ref[...].astype(jnp.float32).T.astype(jnp.bfloat16)
    copies[1].wait()
    unknowns = coarse.shape[1]
    high, low = high_low(coarse[...])
    parts_ref[:, :unknowns] = high
    parts_ref[:, unknowns : 2 * unknowns] = high
    parts_ref[:, 2 * unknowns :] = low
    copies[2].wait()
    for partner, face in enumerate(faces_of_partners()):
        counts_ref[partner : partner + 1, :] = jnp.full((1, counts_ref.shape[1]), rows[0, 0, face], jnp.int32)
    copies[3].wait()


def columns_kernel(*refs):
    field_refs, out_ref = refs[:PARTNERS], refs[PARTNERS]
    for face, ref in zip(faces_of_partners(), field_refs):
        out_ref[face] = ref[...].T


def scale_of(ref):
    depth = ref.shape[0] - SCALE_ROWS
    return ref[depth : depth + 1, :]


def set_scale(ref, scale):
    depth = ref.shape[0] - SCALE_ROWS
    ref[depth:, :] = jnp.broadcast_to(scale, (SCALE_ROWS, scale.shape[1]))


def widest(own_scale, got_refs, counts):
    top = own_scale
    for ref, count in zip(got_refs, counts):
        top = jnp.maximum(top, jnp.where(count > 0, scale_of(ref), own_scale))
    return top


def counts_of(counts_ref):
    return [counts_ref[partner : partner + 1, :] for partner in range(PARTNERS)]


def sum_of_pair(mine_ref, got_ref, depth, top):
    mine, got = mine_ref[:depth, :], got_ref[:depth, :]
    if top is not None:
        mine, got = mine * (scale_of(mine_ref) / top), got * (scale_of(got_ref) / top)
    return mine + got


def coeffs_kernel(scaled, counts_ref, modes_ref, *refs):
    mine_refs, got_refs, out_ref, flat = refs[:4], refs[4:8], refs[8], refs[9]
    counts = counts_of(counts_ref)
    depth = flat.shape[0] // PARTNERS
    top = widest(scale_of(mine_refs[0]), got_refs, counts) if scaled else None
    for face, mine_ref, got_ref, count in zip(faces_of_partners(), mine_refs, got_refs, counts):
        field = masked(sum_of_pair(mine_ref, got_ref, depth, top), count)
        flat[face_slice(face, depth), :] = field.astype(jnp.bfloat16)
    modes = modes_ref.shape[0]
    out_ref[:modes, :] = jnp.dot(modes_ref[...], flat[...], preferred_element_type=jnp.float32)
    if scaled:
        set_scale(out_ref, top)


def base_kernel(scaled, counts_ref, *refs):
    mine_refs, got_refs, part_refs, out_refs = (refs[4 * i : 4 * i + 4] for i in range(4))
    top = scale_of(part_refs[0]) if scaled else None
    depth = mine_refs[0].shape[0] - (SCALE_ROWS if scaled else 0)
    for mine_ref, got_ref, part_ref, out_ref, count in zip(mine_refs, got_refs, part_refs, out_refs, counts_of(counts_ref)):
        out_ref[:depth, :] = masked(sum_of_pair(mine_ref, got_ref, depth, top) - part_ref[:depth, :], count)
        if scaled:
            set_scale(out_ref, top)


def coarse_kernel(cols, scaled, parts_ref, turned_ref, *refs):
    block_refs, out_refs, stack = refs[:cols], refs[cols:-1], refs[-1]
    mine = lax.axis_index("col")
    count = parts_ref.shape[0]
    unknowns = cols * count
    depth = turned_ref.shape[0] // PARTNERS
    top = None
    if scaled:
        top = functools.reduce(jnp.maximum, [scale_of(ref) for ref in block_refs])
    for step, ref in enumerate(block_refs):
        block = ref[:count, :]
        if scaled:
            block = block * (scale_of(ref) / top)
        high, low = high_low(block)
        start = (mine ^ step) * count
        for base, part in ((0, high), (unknowns, low), (2 * unknowns, high)):
            stack[pl.ds(pl.multiple_of(base + start, count), count), :] = part
    coarse = jnp.dot(parts_ref[...], stack[...], preferred_element_type=jnp.float32).astype(jnp.bfloat16)
    for face, out_ref in zip(faces_of_partners(), out_refs):
        out_ref[:depth, :] = jnp.dot(turned_ref[face_slice(face, depth), :], coarse, preferred_element_type=jnp.float32)
        if scaled:
            out_ref[depth:, :] = jnp.broadcast_to(top, (SCALE_ROWS, top.shape[1]))


def dual_rows(operator_ref, flat, face):
    depth = flat.shape[0] // PARTNERS
    return jnp.dot(operator_ref[face_slice(face, depth), :], flat[...], preferred_element_type=jnp.float32) * face_sign(face)


def first_kernel(counts_ref, operator_ref, *refs):
    base_refs, got_part_refs, vector_refs, image_refs = (refs[4 * i : 4 * i + 4] for i in range(4))
    sums_ref, flat = refs[16:]
    faces = faces_of_partners()
    depth = flat.shape[0] // PARTNERS
    norm, curvature, largest = 0.0, 0.0, 0.0
    for face, base_ref, got_ref, vector_ref, count in zip(faces, base_refs, got_part_refs, vector_refs, counts_of(counts_ref)):
        field = base_ref[...] - masked(got_ref[...], count)
        vector_ref[...] = field
        flat[face_slice(face, depth), :] = (field * face_sign(face)).astype(jnp.bfloat16)
        norm += column_sum(field * field)
    for face, vector_ref, image_ref in zip(faces, vector_refs, image_refs):
        value = dual_rows(operator_ref, flat, face)
        image_ref[:depth, :] = value
        curvature += column_sum(vector_ref[...] * value)
        largest = jnp.maximum(largest, jnp.max(jnp.abs(value), axis=0, keepdims=True))
    largest = jnp.where(largest > 0.0, largest, 1.0)
    inverse = 1.0 / largest
    for image_ref in image_refs:
        image_ref[:depth, :] = image_ref[:depth, :] * inverse
        set_scale(image_ref, largest)
    sums_ref[0:1, :] = 0.5 * norm
    sums_ref[1:2, :] = curvature


def second_kernel(counts_ref, operator_ref, sums_in_ref, *refs):
    base_refs, got_part_refs, image_refs, first_refs = (refs[4 * i : 4 * i + 4] for i in range(4))
    after_ref, turned_ref, sums_ref, flat = refs[16:20]
    vector_refs = refs[20:]
    del after_ref
    faces = faces_of_partners()
    counts = counts_of(counts_ref)
    depth = flat.shape[0] // PARTNERS
    own_scale = scale_of(base_refs[0])
    top = widest(own_scale, got_part_refs, counts)
    own_factor = own_scale / top
    mixed, square, reach, bend = 0.0, 0.0, 0.0, 0.0
    for face, base_ref, got_ref, vector_ref, count in zip(faces, base_refs, got_part_refs, vector_refs, counts):
        field = base_ref[:depth, :] * own_factor - masked(got_ref[:depth, :] * (scale_of(got_ref) / top), count)
        vector_ref[...] = field
        flat[face_slice(face, depth), :] = (field * face_sign(face)).astype(jnp.bfloat16)
    for face, vector_ref, first_ref, image_ref in zip(faces, vector_refs, first_refs, image_refs):
        value = dual_rows(operator_ref, flat, face)
        field = vector_ref[...]
        mixed += column_sum(first_ref[...] * field)
        square += column_sum(field * field)
        reach += column_sum(field * image_ref[:depth, :])
        bend += column_sum(field * value)
        turned_ref[face] = field.T
    cross = (2.0 * scale_of(image_refs[0])) * reach
    rows = [sums_in_ref[0:1, :], sums_in_ref[1:2, :], 0.5 * mixed, 0.5 * square, cross, bend, top, top]
    table = jnp.concatenate(rows, axis=0)
    sums_ref[...] = jnp.broadcast_to(table[None], sums_ref.shape)


def last_kernel(sums_ref, first_ref, second_ref, out_hbm, out, sems):
    device = lax.axis_index("col") * lax.axis_size("row") + lax.axis_index("row")
    every = sums_ref[...]
    scales = every[:, 6:7, :]
    top = jnp.max(scales, axis=0, keepdims=True)
    share = scales / top
    norm = jnp.sum(every[:, 0:1, :], axis=0)
    curvature = jnp.sum(every[:, 1:2, :], axis=0)
    mixed = jnp.sum(every[:, 2:3, :] * share, axis=0)
    square = jnp.sum(every[:, 3:4, :] * share * share, axis=0)
    cross = jnp.sum(every[:, 4:5, :] * share, axis=0)
    bend = jnp.sum(every[:, 5:6, :] * share * share, axis=0)
    step = norm / curvature
    reach = step * top[0]
    fresh = norm - 2.0 * reach * mixed + reach * (reach * square)
    ratio = fresh / norm
    grow = 1.0 + ratio
    next_curvature = grow * (grow * curvature) - grow * (reach * cross) + reach * (reach * bend)
    next_step = fresh / next_curvature
    along_first = step + next_step * grow
    along_second = next_step * (step * sums_ref[device, 6:7, :])
    columns = first_ref.shape[1]
    rows = jnp.concatenate([along_first, along_second] + [along_first] * 6, axis=0).T
    copies = []
    pieces = 2
    for piece in range(pieces):
        part = slice(piece * columns // pieces, (piece + 1) * columns // pieces)
        for face in range(PARTNERS):
            out[part, face, :] = rows[part, 0:1] * first_ref[face, part, :] - rows[part, 1:2] * second_ref[face, part, :]
        copies.append(pltpu.make_async_copy(out.at[part], out_hbm.at[part], sems.at[piece]))
        copies[-1].start()
    for copy in copies:
        copy.wait()


VMEM = pl.BlockSpec(memory_space=pltpu.VMEM)
HBM = pl.BlockSpec(memory_space=pltpu.HBM)
ANY = pl.BlockSpec(memory_space=pl.ANY)


def run(kernel, name, outs, scratch, in_specs, args, flops=0, out_spec=VMEM):
    moved = sum(a.size * a.dtype.itemsize for a in args)
    return pl.pallas_call(
        kernel,
        name=name,
        out_shape=outs,
        in_specs=in_specs,
        out_specs=jax.tree.map(lambda _: out_spec, outs),
        scratch_shapes=scratch,
        compiler_params=pltpu.CompilerParams(vmem_limit_bytes=16 * 2**20),
        cost_estimate=pl.CostEstimate(flops=flops, bytes_accessed=moved, transcendentals=0),
    )(*args)


def on_device(rows, cols, local_gap, dual_ops, geneo_modes, coarse_inverse, face_rows):
    tables = swap_tables(rows, cols)
    gap = local_gap[0, 0]
    operator = dual_ops[0, 0]
    modes = geneo_modes[0, 0]
    coarse_block = coarse_inverse[0]
    columns, _, depth = gap.shape
    unknowns = operator.shape[0]
    count = modes.shape[0]

    def shape(*dims, dtype=jnp.float32):
        return jax.ShapeDtypeStruct(dims, dtype)

    def swap(fields):
        return [lax.ppermute(field, ("row", "col"), pairs) for field, pairs in zip(fields, tables)]

    def gather(block):
        steps = [[(c, c ^ step) for c in range(cols)] for step in range(1, cols)]
        return [block] + [lax.ppermute(block, "col", pairs) for pairs in steps]

    def four(height):
        return [shape(height, columns)] * PARTNERS

    flat = pltpu.VMEM((unknowns, columns), jnp.bfloat16)
    wide = pltpu.VMEM((unknowns, columns), jnp.float32)
    tall = depth + SCALE_ROWS

    def in_hbm(array):
        return pltpu.with_memory_space_constraint(array, pltpu.HBM)

    gaps = run(
        gap_kernel, "gap", four(depth), [pltpu.VMEM(gap.shape, gap.dtype), wide, pltpu.SemaphoreType.DMA],
        [HBM], [in_hbm(gap)],
    )
    got_gaps = swap(gaps)
    counts, modes, operator, turned, coarse_parts = run(
        prepare_kernel, "prepare",
        [
            shape(PARTNERS, columns, dtype=jnp.int32),
            shape(*modes.shape, dtype=modes.dtype),
            shape(*operator.shape, dtype=operator.dtype),
            shape(unknowns, count, dtype=modes.dtype),
            shape(count, 3 * cols * count, dtype=jnp.bfloat16),
        ],
        [
            pltpu.SMEM(face_rows.shape, jnp.int32),
            pltpu.VMEM(coarse_block.shape, jnp.float32),
            pltpu.SemaphoreType.DMA((4,)),
        ],
        [HBM] * 4 + [ANY], [*map(in_hbm, (face_rows, modes, coarse_block, operator)), gaps[PARTNERS - 1]],
    )
    stack = pltpu.VMEM((3 * cols * count, columns), jnp.bfloat16)

    def correction(scaled, fields, got_fields):
        extra = SCALE_ROWS if scaled else 0
        name = "second" if scaled else "first"
        coeffs = run(
            functools.partial(coeffs_kernel, scaled), name + "_coeffs", shape(count + extra, columns), [flat],
            [VMEM] * 10, [counts, modes, *fields, *got_fields],
        )
        parts = run(
            functools.partial(coarse_kernel, cols, scaled), name + "_coarse", four(depth + extra), [stack],
            [VMEM] * (2 + cols), [coarse_parts, turned, *gather(coeffs)],
        )
        got_parts = swap(parts)
        base = run(
            functools.partial(base_kernel, scaled), name + "_base", four(depth + extra), [],
            [VMEM] * 13, [counts, *fields, *got_fields, *parts],
        )
        return base, got_parts

    base, got_parts = correction(False, gaps, got_gaps)
    *first, sums = run(
        first_kernel, "first", four(depth) + four(tall) + [shape(2, columns)], [flat],
        [VMEM] * 10, [counts, operator, *base, *got_parts],
    )
    first, images = first[:PARTNERS], first[PARTNERS:]
    got_images = swap(images)
    first_turned = run(columns_kernel, "columns", shape(PARTNERS, columns, depth), [], [VMEM] * 4, first)
    base, got_parts = correction(True, images, got_images)
    second_turned, sums = run(
        second_kernel, "second", [shape(PARTNERS, columns, depth), shape(rows * cols, 8, columns)],
        [flat] + [pltpu.VMEM((depth, columns), jnp.float32)] * PARTNERS,
        [VMEM] * 19 + [ANY], [counts, operator, sums, *base, *got_parts, *images, *first, first_turned],
    )
    every = lax.all_to_all(sums, ("col", "row"), 0, 0)
    whole = (columns, PARTNERS, depth)
    out = run(
        last_kernel, "last", shape(*whole),
        [pltpu.VMEM(whole, jnp.float32), pltpu.SemaphoreType.DMA((2,))],
        [VMEM] * 3, [every, first_turned, second_turned], out_spec=HBM,
    )
    return out[None, None]


def solution(mesh):
    rows, cols = mesh.shape["row"], mesh.shape["col"]

    def body(*arrays):
        return on_device(rows, cols, *arrays)

    return jax.shard_map(
        body,
        mesh=mesh,
        in_specs=(
            P("row", "col", None, None, None),
            P("row", "col", None, None),
            P("row", "col", None, None),
            P("row", "col", None),
            P("row", "col", None),
        ),
        out_specs=P("row", "col", None, None, None),
        check_vma=False,
    )
```

```python
import functools

import jax
import jax.numpy as jnp
from jax import lax
from jax.experimental import pallas as pl
from jax.experimental.pallas import tpu as pltpu
from jax.sharding import PartitionSpec as P

PARTNERS = 4
SCALE_ROWS = 8


def swap_tables(rows, cols):
    def table(partner):
        pairs = []
        for r in range(rows):
            for c in range(cols):
                r2, c2 = partner(r, c)
                pairs.append((r * cols + c, r2 * cols + c2))
        return pairs

    def idle(c):
        return c - c % 4 + (1, 3, 0, 2)[c % 4] if cols % 4 == 0 else c ^ 1

    def across_rows(r, c):
        other = r + 1 if r % 2 else r - 1
        return (other, c) if 0 <= other < rows else (r, idle(c))

    def across_cols(r, c):
        other = c + 1 if c % 2 else c - 1
        return (r, other) if 0 <= other < cols else (r ^ 1, c)

    return [
        table(across_cols),
        table(lambda r, c: (r, c ^ 1)),
        table(across_rows),
        table(lambda r, c: (r ^ 1, c)),
    ]


def faces_of_partners():
    odd_row = lax.rem(lax.axis_index("row"), 2)
    odd_col = lax.rem(lax.axis_index("col"), 2)
    return [2 + odd_col, 3 - odd_col, odd_row, 1 - odd_row]


def face_slice(face, depth):
    return pl.ds(pl.multiple_of(face * depth, depth), depth)


def face_sign(face):
    return (2 * lax.rem(face, 2) - 1).astype(jnp.float32)


def masked(value, count):
    unknown = lax.broadcasted_iota(jnp.int32, value.shape, 0)
    return jnp.where(unknown < count, value, 0.0)


def column_sum(value):
    return jnp.sum(value, axis=0, keepdims=True)


def gap_kernel(gap_hbm, *refs):
    out_refs, (gap, field, sem) = refs[:PARTNERS], refs[PARTNERS:]
    copy = pltpu.make_async_copy(gap_hbm, gap, sem)
    copy.start()
    copy.wait()
    depth = gap.shape[2]
    for face in range(PARTNERS):
        sign = 1.0 if face % 2 else -1.0
        block = gap[:, face, :].astype(jnp.float32) * sign
        field[face * depth : (face + 1) * depth, :] = block.T
    for face, out_ref in zip(faces_of_partners(), out_refs):
        out_ref[...] = field[face_slice(face, depth), :]


def high_low(value):
    high = value.astype(jnp.bfloat16)
    return high, (value - high.astype(jnp.float32)).astype(jnp.bfloat16)


def prepare_kernel(rows_hbm, modes_hbm, coarse_hbm, operator_hbm, after_ref, *refs):
    del after_ref
    counts_ref, modes_ref, operator_ref, turned_ref, parts_ref, rows, coarse, sems = refs
    moves = [(modes_hbm, modes_ref), (coarse_hbm, coarse), (rows_hbm, rows), (operator_hbm, operator_ref)]
    copies = [pltpu.make_async_copy(source, target, sems.at[at]) for at, (source, target) in enumerate(moves)]
    for copy in copies:
        copy.start()
    copies[0].wait()
    turned_ref[...] = modes_ref[...].astype(jnp.float32).T.astype(jnp.bfloat16)
    copies[1].wait()
    unknowns = coarse.shape[1]
    high, low = high_low(coarse[...])
    parts_ref[:, :unknowns] = high
    parts_ref[:, unknowns : 2 * unknowns] = high
    parts_ref[:, 2 * unknowns :] = low
    copies[2].wait()
    for partner, face in enumerate(faces_of_partners()):
        counts_ref[partner : partner + 1, :] = jnp.full((1, counts_ref.shape[1]), rows[0, 0, face], jnp.int32)
    copies[3].wait()


def columns_kernel(*refs):
    field_refs, out_ref = refs[:PARTNERS], refs[PARTNERS]
    for face, ref in zip(faces_of_partners(), field_refs):
        out_ref[face] = ref[...].T


def scale_of(ref):
    depth = ref.shape[0] - SCALE_ROWS
    return ref[depth : depth + 1, :]


def set_scale(ref, scale):
    depth = ref.shape[0] - SCALE_ROWS
    ref[depth:, :] = jnp.broadcast_to(scale, (SCALE_ROWS, scale.shape[1]))


def widest(own_scale, got_refs, counts):
    top = own_scale
    for ref, count in zip(got_refs, counts):
        top = jnp.maximum(top, jnp.where(count > 0, scale_of(ref), own_scale))
    return top


def counts_of(counts_ref):
    return [counts_ref[partner : partner + 1, :] for partner in range(PARTNERS)]


def sum_of_pair(mine_ref, got_ref, depth, top):
    mine, got = mine_ref[:depth, :], got_ref[:depth, :]
    total = mine + got
    return total if top is None else total * (1.0 / top)


def coeffs_kernel(scaled, counts_ref, modes_ref, *refs):
    mine_refs, got_refs, out_ref, flat = refs[:4], refs[4:8], refs[8], refs[9]
    counts = counts_of(counts_ref)
    depth = flat.shape[0] // PARTNERS
    top = widest(scale_of(mine_refs[0]), got_refs, counts) if scaled else None
    for face, mine_ref, got_ref, count in zip(faces_of_partners(), mine_refs, got_refs, counts):
        field = masked(sum_of_pair(mine_ref, got_ref, depth, top), count)
        flat[face_slice(face, depth), :] = field.astype(jnp.bfloat16)
    modes = modes_ref.shape[0]
    out_ref[:modes, :] = jnp.dot(modes_ref[...], flat[...], preferred_element_type=jnp.float32)
    if scaled:
        set_scale(out_ref, top)


def base_kernel(scaled, counts_ref, *refs):
    mine_refs, got_refs, part_refs, out_refs = (refs[4 * i : 4 * i + 4] for i in range(4))
    top = scale_of(part_refs[0]) if scaled else None
    depth = mine_refs[0].shape[0] - (SCALE_ROWS if scaled else 0)
    for mine_ref, got_ref, part_ref, out_ref, count in zip(mine_refs, got_refs, part_refs, out_refs, counts_of(counts_ref)):
        out_ref[:depth, :] = masked(sum_of_pair(mine_ref, got_ref, depth, top) - part_ref[:depth, :], count)
        if scaled:
            set_scale(out_ref, top)


def coarse_kernel(cols, scaled, parts_ref, turned_ref, *refs):
    block_refs, out_refs, stack = refs[:cols], refs[cols:-1], refs[-1]
    mine = lax.axis_index("col")
    count = parts_ref.shape[0]
    unknowns = cols * count
    depth = turned_ref.shape[0] // PARTNERS
    top = None
    if scaled:
        top = functools.reduce(jnp.maximum, [scale_of(ref) for ref in block_refs])
    for step, ref in enumerate(block_refs):
        block = ref[:count, :]
        if scaled:
            block = block * (scale_of(ref) / top)
        high, low = high_low(block)
        start = (mine ^ step) * count
        for base, part in ((0, high), (unknowns, low), (2 * unknowns, high)):
            stack[pl.ds(pl.multiple_of(base + start, count), count), :] = part
    coarse = jnp.dot(parts_ref[...], stack[...], preferred_element_type=jnp.float32).astype(jnp.bfloat16)
    for face, out_ref in zip(faces_of_partners(), out_refs):
        out_ref[:depth, :] = jnp.dot(turned_ref[face_slice(face, depth), :], coarse, preferred_element_type=jnp.float32)
        if scaled:
            out_ref[depth:, :] = jnp.broadcast_to(top, (SCALE_ROWS, top.shape[1]))


def dual_rows(operator_ref, flat, face):
    depth = flat.shape[0] // PARTNERS
    return jnp.dot(operator_ref[face_slice(face, depth), :], flat[...], preferred_element_type=jnp.float32) * face_sign(face)


def first_kernel(counts_ref, operator_ref, *refs):
    base_refs, got_part_refs, vector_refs, image_refs = (refs[4 * i : 4 * i + 4] for i in range(4))
    sums_ref, flat = refs[16:]
    faces = faces_of_partners()
    depth = flat.shape[0] // PARTNERS
    norm, curvature, largest = 0.0, 0.0, 0.0
    for face, base_ref, got_ref, vector_ref, count in zip(faces, base_refs, got_part_refs, vector_refs, counts_of(counts_ref)):
        field = base_ref[...] - masked(got_ref[...], count)
        vector_ref[...] = field
        flat[face_slice(face, depth), :] = (field * face_sign(face)).astype(jnp.bfloat16)
        norm += column_sum(field * field)
    for face, vector_ref, image_ref in zip(faces, vector_refs, image_refs):
        value = dual_rows(operator_ref, flat, face)
        image_ref[:depth, :] = value
        curvature += column_sum(vector_ref[...] * value)
        largest = jnp.maximum(largest, jnp.max(jnp.abs(value), axis=0, keepdims=True))
    largest = jnp.where(largest > 0.0, largest, 1.0)
    for image_ref in image_refs:
        set_scale(image_ref, largest)
    sums_ref[0:1, :] = 0.5 * norm
    sums_ref[1:2, :] = curvature


def second_kernel(counts_ref, operator_ref, sums_in_ref, *refs):
    base_refs, got_part_refs, image_refs, first_refs = (refs[4 * i : 4 * i + 4] for i in range(4))
    after_ref, turned_ref, sums_ref, flat = refs[16:20]
    vector_refs = refs[20:]
    del after_ref
    faces = faces_of_partners()
    counts = counts_of(counts_ref)
    depth = flat.shape[0] // PARTNERS
    own_scale = scale_of(base_refs[0])
    top = widest(own_scale, got_part_refs, counts)
    own_factor = own_scale / top
    inverse = 1.0 / scale_of(image_refs[0])
    mixed, square, reach, bend = 0.0, 0.0, 0.0, 0.0
    for face, base_ref, got_ref, vector_ref, count in zip(faces, base_refs, got_part_refs, vector_refs, counts):
        field = base_ref[:depth, :] * own_factor - masked(got_ref[:depth, :] * (scale_of(got_ref) / top), count)
        vector_ref[...] = field
        flat[face_slice(face, depth), :] = (field * face_sign(face)).astype(jnp.bfloat16)
    for face, vector_ref, first_ref, image_ref in zip(faces, vector_refs, first_refs, image_refs):
        value = dual_rows(operator_ref, flat, face)
        field = vector_ref[...]
        mixed += column_sum(first_ref[...] * field)
        square += column_sum(field * field)
        reach += column_sum(field * (image_ref[:depth, :] * inverse))
        bend += column_sum(field * value)
        turned_ref[face] = field.T
    cross = (2.0 * scale_of(image_refs[0])) * reach
    rows = [sums_in_ref[0:1, :], sums_in_ref[1:2, :], 0.5 * mixed, 0.5 * square, cross, bend, top, top]
    table = jnp.concatenate(rows, axis=0)
    sums_ref[...] = jnp.broadcast_to(table[None], sums_ref.shape)


def last_kernel(sums_ref, first_ref, second_ref, out_hbm, out, sems):
    device = lax.axis_index("col") * lax.axis_size("row") + lax.axis_index("row")
    every = sums_ref[...]
    scales = every[:, 6:7, :]
    top = jnp.max(scales, axis=0, keepdims=True)
    share = scales / top
    norm = jnp.sum(every[:, 0:1, :], axis=0)
    curvature = jnp.sum(every[:, 1:2, :], axis=0)
    mixed = jnp.sum(every[:, 2:3, :] * share, axis=0)
    square = jnp.sum(every[:, 3:4, :] * share * share, axis=0)
    cross = jnp.sum(every[:, 4:5, :] * share, axis=0)
    bend = jnp.sum(every[:, 5:6, :] * share * share, axis=0)
    step = norm / curvature
    reach = step * top[0]
    fresh = norm - 2.0 * reach * mixed + reach * (reach * square)
    ratio = fresh / norm
    grow = 1.0 + ratio
    next_curvature = grow * (grow * curvature) - grow * (reach * cross) + reach * (reach * bend)
    next_step = fresh / next_curvature
    along_first = step + next_step * grow
    along_second = next_step * (step * sums_ref[device, 6:7, :])
    columns = first_ref.shape[1]
    rows = jnp.concatenate([along_first, along_second] + [along_first] * 6, axis=0).T
    copies = []
    pieces = 2
    for piece in range(pieces):
        part = slice(piece * columns // pieces, (piece + 1) * columns // pieces)
        for face in range(PARTNERS):
            out[part, face, :] = rows[part, 0:1] * first_ref[face, part, :] - rows[part, 1:2] * second_ref[face, part, :]
        copies.append(pltpu.make_async_copy(out.at[part], out_hbm.at[part], sems.at[piece]))
        copies[-1].start()
    for copy in copies:
        copy.wait()


VMEM = pl.BlockSpec(memory_space=pltpu.VMEM)
HBM = pl.BlockSpec(memory_space=pltpu.HBM)
ANY = pl.BlockSpec(memory_space=pl.ANY)


def run(kernel, name, outs, scratch, in_specs, args, flops=0, out_spec=VMEM):
    moved = sum(a.size * a.dtype.itemsize for a in args)
    return pl.pallas_call(
        kernel,
        name=name,
        out_shape=outs,
        in_specs=in_specs,
        out_specs=jax.tree.map(lambda _: out_spec, outs),
        scratch_shapes=scratch,
        compiler_params=pltpu.CompilerParams(vmem_limit_bytes=16 * 2**20),
        cost_estimate=pl.CostEstimate(flops=flops, bytes_accessed=moved, transcendentals=0),
    )(*args)


def on_device(rows, cols, local_gap, dual_ops, geneo_modes, coarse_inverse, face_rows):
    tables = swap_tables(rows, cols)
    gap = local_gap[0, 0]
    operator = dual_ops[0, 0]
    modes = geneo_modes[0, 0]
    coarse_block = coarse_inverse[0]
    columns, _, depth = gap.shape
    unknowns = operator.shape[0]
    count = modes.shape[0]

    def shape(*dims, dtype=jnp.float32):
        return jax.ShapeDtypeStruct(dims, dtype)

    def swap(fields):
        return [lax.ppermute(field, ("row", "col"), pairs) for field, pairs in zip(fields, tables)]

    def gather(block):
        steps = [[(c, c ^ step) for c in range(cols)] for step in range(1, cols)]
        return [block] + [lax.ppermute(block, "col", pairs) for pairs in steps]

    def four(height):
        return [shape(height, columns)] * PARTNERS

    flat = pltpu.VMEM((unknowns, columns), jnp.bfloat16)
    wide = pltpu.VMEM((unknowns, columns), jnp.float32)
    tall = depth + SCALE_ROWS

    def in_hbm(array):
        return pltpu.with_memory_space_constraint(array, pltpu.HBM)

    gaps = run(
        gap_kernel, "gap", four(depth), [pltpu.VMEM(gap.shape, gap.dtype), wide, pltpu.SemaphoreType.DMA],
        [HBM], [in_hbm(gap)],
    )
    got_gaps = swap(gaps)
    counts, modes, operator, turned, coarse_parts = run(
        prepare_kernel, "prepare",
        [
            shape(PARTNERS, columns, dtype=jnp.int32),
            shape(*modes.shape, dtype=modes.dtype),
            shape(*operator.shape, dtype=operator.dtype),
            shape(unknowns, count, dtype=modes.dtype),
            shape(count, 3 * cols * count, dtype=jnp.bfloat16),
        ],
        [
            pltpu.SMEM(face_rows.shape, jnp.int32),
            pltpu.VMEM(coarse_block.shape, jnp.float32),
            pltpu.SemaphoreType.DMA((4,)),
        ],
        [HBM] * 4 + [ANY], [*map(in_hbm, (face_rows, modes, coarse_block, operator)), gaps[PARTNERS - 1]],
    )
    stack = pltpu.VMEM((3 * cols * count, columns), jnp.bfloat16)

    def correction(scaled, fields, got_fields):
        extra = SCALE_ROWS if scaled else 0
        name = "second" if scaled else "first"
        coeffs = run(
            functools.partial(coeffs_kernel, scaled), name + "_coeffs", shape(count + extra, columns), [flat],
            [VMEM] * 10, [counts, modes, *fields, *got_fields],
        )
        parts = run(
            functools.partial(coarse_kernel, cols, scaled), name + "_coarse", four(depth + extra), [stack],
            [VMEM] * (2 + cols), [coarse_parts, turned, *gather(coeffs)],
        )
        got_parts = swap(parts)
        base = run(
            functools.partial(base_kernel, scaled), name + "_base", four(depth + extra), [],
            [VMEM] * 13, [counts, *fields, *got_fields, *parts],
        )
        return base, got_parts

    base, got_parts = correction(False, gaps, got_gaps)
    *first, sums = run(
        first_kernel, "first", four(depth) + four(tall) + [shape(2, columns)], [flat],
        [VMEM] * 10, [counts, operator, *base, *got_parts],
    )
    first, images = first[:PARTNERS], first[PARTNERS:]
    got_images = swap(images)
    first_turned = run(columns_kernel, "columns", shape(PARTNERS, columns, depth), [], [VMEM] * 4, first)
    base, got_parts = correction(True, images, got_images)
    second_turned, sums = run(
        second_kernel, "second", [shape(PARTNERS, columns, depth), shape(rows * cols, 8, columns)],
        [flat] + [pltpu.VMEM((depth, columns), jnp.float32)] * PARTNERS,
        [VMEM] * 19 + [ANY], [counts, operator, sums, *base, *got_parts, *images, *first, first_turned],
    )
    every = lax.all_to_all(sums, ("col", "row"), 0, 0)
    whole = (columns, PARTNERS, depth)
    out = run(
        last_kernel, "last", shape(*whole),
        [pltpu.VMEM(whole, jnp.float32), pltpu.SemaphoreType.DMA((2,))],
        [VMEM] * 3, [every, first_turned, second_turned], out_spec=HBM,
    )
    return out[None, None]


def solution(mesh):
    rows, cols = mesh.shape["row"], mesh.shape["col"]

    def body(*arrays):
        return on_device(rows, cols, *arrays)

    return jax.shard_map(
        body,
        mesh=mesh,
        in_specs=(
            P("row", "col", None, None, None),
            P("row", "col", None, None),
            P("row", "col", None, None),
            P("row", "col", None),
            P("row", "col", None),
        ),
        out_specs=P("row", "col", None, None, None),
        check_vma=False,
    )
```

```python
import functools

import jax
import jax.numpy as jnp
from jax import lax
from jax.experimental import pallas as pl
from jax.experimental.pallas import tpu as pltpu
from jax.sharding import PartitionSpec as P

PARTNERS = 4
SCALE_ROWS = 8


def swap_tables(rows, cols):
    def table(partner):
        pairs = []
        for r in range(rows):
            for c in range(cols):
                r2, c2 = partner(r, c)
                pairs.append((r * cols + c, r2 * cols + c2))
        return pairs

    def idle(c):
        return c - c % 4 + (1, 3, 0, 2)[c % 4] if cols % 4 == 0 else c ^ 1

    def across_rows(r, c):
        other = r + 1 if r % 2 else r - 1
        return (other, c) if 0 <= other < rows else (r, idle(c))

    def across_cols(r, c):
        other = c + 1 if c % 2 else c - 1
        return (r, other) if 0 <= other < cols else (r ^ 1, c)

    return [
        table(across_cols),
        table(lambda r, c: (r, c ^ 1)),
        table(across_rows),
        table(lambda r, c: (r ^ 1, c)),
    ]


def faces_of_partners():
    odd_row = lax.rem(lax.axis_index("row"), 2)
    odd_col = lax.rem(lax.axis_index("col"), 2)
    return [2 + odd_col, 3 - odd_col, odd_row, 1 - odd_row]


def face_slice(face, depth):
    return pl.ds(pl.multiple_of(face * depth, depth), depth)


def face_sign(face):
    return (2 * lax.rem(face, 2) - 1).astype(jnp.float32)


def masked(value, count):
    unknown = lax.broadcasted_iota(jnp.int32, value.shape, 0)
    return jnp.where(unknown < count, value, 0.0)


def column_sum(value):
    return jnp.sum(value.reshape(-1, 8, value.shape[1]), axis=0)


def column_total(partial_sums):
    return jnp.sum(partial_sums, axis=0, keepdims=True)


def gap_kernel(gap_hbm, *refs):
    out_refs, (gap, field, sem) = refs[:PARTNERS], refs[PARTNERS:]
    copy = pltpu.make_async_copy(gap_hbm, gap, sem)
    copy.start()
    copy.wait()
    depth = gap.shape[2]
    for face in range(PARTNERS):
        sign = 1.0 if face % 2 else -1.0
        block = gap[:, face, :].astype(jnp.float32) * sign
        field[face * depth : (face + 1) * depth, :] = block.T
    for face, out_ref in zip(faces_of_partners(), out_refs):
        out_ref[...] = field[face_slice(face, depth), :]


def high_low(value):
    high = value.astype(jnp.bfloat16)
    return high, (value - high.astype(jnp.float32)).astype(jnp.bfloat16)


def prepare_kernel(rows_hbm, modes_hbm, coarse_hbm, operator_hbm, after_ref, *refs):
    del after_ref
    counts_ref, modes_ref, operator_ref, turned_ref, parts_ref, rows, coarse, sems = refs
    moves = [(modes_hbm, modes_ref), (coarse_hbm, coarse), (rows_hbm, rows), (operator_hbm, operator_ref)]
    copies = [pltpu.make_async_copy(source, target, sems.at[at]) for at, (source, target) in enumerate(moves)]
    for copy in copies:
        copy.start()
    copies[0].wait()
    turned_ref[...] = modes_ref[...].astype(jnp.float32).T.astype(jnp.bfloat16)
    copies[1].wait()
    unknowns = coarse.shape[1]
    high, low = high_low(coarse[...])
    parts_ref[:, :unknowns] = high
    parts_ref[:, unknowns : 2 * unknowns] = high
    parts_ref[:, 2 * unknowns :] = low
    copies[2].wait()
    for partner, face in enumerate(faces_of_partners()):
        counts_ref[partner : partner + 1, :] = jnp.full((1, counts_ref.shape[1]), rows[0, 0, face], jnp.int32)
    copies[3].wait()


def columns_kernel(*refs):
    field_refs, out_ref = refs[:PARTNERS], refs[PARTNERS]
    for face, ref in zip(faces_of_partners(), field_refs):
        out_ref[face] = ref[...].T


def scale_of(ref):
    depth = ref.shape[0] - SCALE_ROWS
    return ref[depth : depth + 1, :]


def set_scale(ref, scale):
    depth = ref.shape[0] - SCALE_ROWS
    ref[depth:, :] = jnp.broadcast_to(scale, (SCALE_ROWS, scale.shape[1]))


def widest(own_scale, got_refs, counts):
    top = own_scale
    for ref, count in zip(got_refs, counts):
        top = jnp.maximum(top, jnp.where(count > 0, scale_of(ref), own_scale))
    return top


def counts_of(counts_ref):
    return [counts_ref[partner : partner + 1, :] for partner in range(PARTNERS)]


def sum_of_pair(mine_ref, got_ref, depth, top):
    mine, got = mine_ref[:depth, :], got_ref[:depth, :]
    total = mine + got
    return total if top is None else total * (1.0 / top)


def coeffs_kernel(scaled, counts_ref, modes_ref, *refs):
    mine_refs, got_refs, out_ref, flat = refs[:4], refs[4:8], refs[8], refs[9]
    counts = counts_of(counts_ref)
    depth = flat.shape[0] // PARTNERS
    top = widest(scale_of(mine_refs[0]), got_refs, counts) if scaled else None
    for face, mine_ref, got_ref, count in zip(faces_of_partners(), mine_refs, got_refs, counts):
        field = masked(sum_of_pair(mine_ref, got_ref, depth, top), count)
        flat[face_slice(face, depth), :] = field.astype(jnp.bfloat16)
    modes = modes_ref.shape[0]
    out_ref[:modes, :] = jnp.dot(modes_ref[...], flat[...], preferred_element_type=jnp.float32)
    if scaled:
        set_scale(out_ref, top)


def base_kernel(scaled, counts_ref, *refs):
    mine_refs, got_refs, part_refs, out_refs = (refs[4 * i : 4 * i + 4] for i in range(4))
    top = scale_of(part_refs[0]) if scaled else None
    depth = mine_refs[0].shape[0] - (SCALE_ROWS if scaled else 0)
    for mine_ref, got_ref, part_ref, out_ref, count in zip(mine_refs, got_refs, part_refs, out_refs, counts_of(counts_ref)):
        out_ref[:depth, :] = masked(sum_of_pair(mine_ref, got_ref, depth, top) - part_ref[:depth, :], count)
        if scaled:
            set_scale(out_ref, top)


def coarse_kernel(cols, scaled, parts_ref, turned_ref, *refs):
    block_refs, out_refs, stack = refs[:cols], refs[cols:-1], refs[-1]
    mine = lax.axis_index("col")
    count = parts_ref.shape[0]
    unknowns = cols * count
    depth = turned_ref.shape[0] // PARTNERS
    top = None
    if scaled:
        top = functools.reduce(jnp.maximum, [scale_of(ref) for ref in block_refs])
    for step, ref in enumerate(block_refs):
        block = ref[:count, :]
        if scaled:
            block = block * (scale_of(ref) / top)
        high, low = high_low(block)
        start = (mine ^ step) * count
        for base, part in ((0, high), (unknowns, low), (2 * unknowns, high)):
            stack[pl.ds(pl.multiple_of(base + start, count), count), :] = part
    coarse = jnp.dot(parts_ref[...], stack[...], preferred_element_type=jnp.float32).astype(jnp.bfloat16)
    for face, out_ref in zip(faces_of_partners(), out_refs):
        out_ref[:depth, :] = jnp.dot(turned_ref[face_slice(face, depth), :], coarse, preferred_element_type=jnp.float32)
        if scaled:
            out_ref[depth:, :] = jnp.broadcast_to(top, (SCALE_ROWS, top.shape[1]))


def dual_rows(operator_ref, flat, face):
    depth = flat.shape[0] // PARTNERS
    return jnp.dot(operator_ref[face_slice(face, depth), :], flat[...], preferred_element_type=jnp.float32) * face_sign(face)


def first_kernel(counts_ref, operator_ref, *refs):
    base_refs, got_part_refs, vector_refs, image_refs = (refs[4 * i : 4 * i + 4] for i in range(4))
    sums_ref, flat = refs[16:]
    faces = faces_of_partners()
    depth = flat.shape[0] // PARTNERS
    norm, curvature, largest = 0.0, 0.0, 0.0
    for face, base_ref, got_ref, vector_ref, count in zip(faces, base_refs, got_part_refs, vector_refs, counts_of(counts_ref)):
        field = base_ref[...] - masked(got_ref[...], count)
        vector_ref[...] = field
        flat[face_slice(face, depth), :] = (field * face_sign(face)).astype(jnp.bfloat16)
        norm += column_sum(field * field)
    for face, vector_ref, image_ref in zip(faces, vector_refs, image_refs):
        value = dual_rows(operator_ref, flat, face)
        image_ref[:depth, :] = value
        curvature += column_sum(vector_ref[...] * value)
        largest = jnp.maximum(largest, jnp.max(jnp.abs(value), axis=0, keepdims=True))
    largest = jnp.where(largest > 0.0, largest, 1.0)
    for image_ref in image_refs:
        set_scale(image_ref, largest)
    sums_ref[0:1, :] = 0.5 * column_total(norm)
    sums_ref[1:2, :] = column_total(curvature)


def second_kernel(counts_ref, operator_ref, sums_in_ref, *refs):
    base_refs, got_part_refs, image_refs, first_refs = (refs[4 * i : 4 * i + 4] for i in range(4))
    after_ref, turned_ref, sums_ref, flat = refs[16:20]
    vector_refs = refs[20:]
    del after_ref
    faces = faces_of_partners()
    counts = counts_of(counts_ref)
    depth = flat.shape[0] // PARTNERS
    own_scale = scale_of(base_refs[0])
    top = widest(own_scale, got_part_refs, counts)
    own_factor = own_scale / top
    inverse = 1.0 / scale_of(image_refs[0])
    mixed, square, reach, bend = 0.0, 0.0, 0.0, 0.0
    for face, base_ref, got_ref, vector_ref, count in zip(faces, base_refs, got_part_refs, vector_refs, counts):
        field = base_ref[:depth, :] * own_factor - masked(got_ref[:depth, :] * (scale_of(got_ref) / top), count)
        vector_ref[...] = field
        flat[face_slice(face, depth), :] = (field * face_sign(face)).astype(jnp.bfloat16)
    for face, vector_ref, first_ref, image_ref in zip(faces, vector_refs, first_refs, image_refs):
        value = dual_rows(operator_ref, flat, face)
        field = vector_ref[...]
        mixed += column_sum(first_ref[...] * field)
        square += column_sum(field * field)
        reach += column_sum(field * (image_ref[:depth, :] * inverse))
        bend += column_sum(field * value)
        turned_ref[face] = field.T
    mixed, square, reach, bend = map(column_total, (mixed, square, reach, bend))
    cross = (2.0 * scale_of(image_refs[0])) * reach
    rows = [sums_in_ref[0:1, :], sums_in_ref[1:2, :], 0.5 * mixed, 0.5 * square, cross, bend, top, top]
    table = jnp.concatenate(rows, axis=0)
    sums_ref[...] = jnp.broadcast_to(table[None], sums_ref.shape)


def last_kernel(sums_ref, first_ref, second_ref, out_hbm, out, sems):
    device = lax.axis_index("col") * lax.axis_size("row") + lax.axis_index("row")
    every = sums_ref[...]
    scales = every[:, 6:7, :]
    top = jnp.max(scales, axis=0, keepdims=True)
    share = scales / top
    norm = jnp.sum(every[:, 0:1, :], axis=0)
    curvature = jnp.sum(every[:, 1:2, :], axis=0)
    mixed = jnp.sum(every[:, 2:3, :] * share, axis=0)
    square = jnp.sum(every[:, 3:4, :] * share * share, axis=0)
    cross = jnp.sum(every[:, 4:5, :] * share, axis=0)
    bend = jnp.sum(every[:, 5:6, :] * share * share, axis=0)
    step = norm / curvature
    reach = step * top[0]
    fresh = norm - 2.0 * reach * mixed + reach * (reach * square)
    ratio = fresh / norm
    grow = 1.0 + ratio
    next_curvature = grow * (grow * curvature) - grow * (reach * cross) + reach * (reach * bend)
    next_step = fresh / next_curvature
    along_first = step + next_step * grow
    along_second = next_step * (step * sums_ref[device, 6:7, :])
    columns = first_ref.shape[1]
    rows = jnp.concatenate([along_first, along_second] + [along_first] * 6, axis=0).T
    copies = []
    pieces = 2
    for piece in range(pieces):
        part = slice(piece * columns // pieces, (piece + 1) * columns // pieces)
        for face in range(PARTNERS):
            out[part, face, :] = rows[part, 0:1] * first_ref[face, part, :] - rows[part, 1:2] * second_ref[face, part, :]
        copies.append(pltpu.make_async_copy(out.at[part], out_hbm.at[part], sems.at[piece]))
        copies[-1].start()
    for copy in copies:
        copy.wait()


VMEM = pl.BlockSpec(memory_space=pltpu.VMEM)
HBM = pl.BlockSpec(memory_space=pltpu.HBM)
ANY = pl.BlockSpec(memory_space=pl.ANY)


def run(kernel, name, outs, scratch, in_specs, args, flops=0, out_spec=VMEM):
    moved = sum(a.size * a.dtype.itemsize for a in args)
    return pl.pallas_call(
        kernel,
        name=name,
        out_shape=outs,
        in_specs=in_specs,
        out_specs=jax.tree.map(lambda _: out_spec, outs),
        scratch_shapes=scratch,
        compiler_params=pltpu.CompilerParams(vmem_limit_bytes=16 * 2**20),
        cost_estimate=pl.CostEstimate(flops=flops, bytes_accessed=moved, transcendentals=0),
    )(*args)


def on_device(rows, cols, local_gap, dual_ops, geneo_modes, coarse_inverse, face_rows):
    tables = swap_tables(rows, cols)
    gap = local_gap[0, 0]
    operator = dual_ops[0, 0]
    modes = geneo_modes[0, 0]
    coarse_block = coarse_inverse[0]
    columns, _, depth = gap.shape
    unknowns = operator.shape[0]
    count = modes.shape[0]

    def shape(*dims, dtype=jnp.float32):
        return jax.ShapeDtypeStruct(dims, dtype)

    def swap(fields):
        return [lax.ppermute(field, ("row", "col"), pairs) for field, pairs in zip(fields, tables)]

    def gather(block):
        steps = [[(c, c ^ step) for c in range(cols)] for step in range(1, cols)]
        return [block] + [lax.ppermute(block, "col", pairs) for pairs in steps]

    def four(height):
        return [shape(height, columns)] * PARTNERS

    flat = pltpu.VMEM((unknowns, columns), jnp.bfloat16)
    wide = pltpu.VMEM((unknowns, columns), jnp.float32)
    tall = depth + SCALE_ROWS

    def in_hbm(array):
        return pltpu.with_memory_space_constraint(array, pltpu.HBM)

    gaps = run(
        gap_kernel, "gap", four(depth), [pltpu.VMEM(gap.shape, gap.dtype), wide, pltpu.SemaphoreType.DMA],
        [HBM], [in_hbm(gap)],
    )
    got_gaps = swap(gaps)
    counts, modes, operator, turned, coarse_parts = run(
        prepare_kernel, "prepare",
        [
            shape(PARTNERS, columns, dtype=jnp.int32),
            shape(*modes.shape, dtype=modes.dtype),
            shape(*operator.shape, dtype=operator.dtype),
            shape(unknowns, count, dtype=modes.dtype),
            shape(count, 3 * cols * count, dtype=jnp.bfloat16),
        ],
        [
            pltpu.SMEM(face_rows.shape, jnp.int32),
            pltpu.VMEM(coarse_block.shape, jnp.float32),
            pltpu.SemaphoreType.DMA((4,)),
        ],
        [HBM] * 4 + [ANY], [*map(in_hbm, (face_rows, modes, coarse_block, operator)), gaps[PARTNERS - 1]],
    )
    stack = pltpu.VMEM((3 * cols * count, columns), jnp.bfloat16)

    def correction(scaled, fields, got_fields):
        extra = SCALE_ROWS if scaled else 0
        name = "second" if scaled else "first"
        coeffs = run(
            functools.partial(coeffs_kernel, scaled), name + "_coeffs", shape(count + extra, columns), [flat],
            [VMEM] * 10, [counts, modes, *fields, *got_fields],
        )
        parts = run(
            functools.partial(coarse_kernel, cols, scaled), name + "_coarse", four(depth + extra), [stack],
            [VMEM] * (2 + cols), [coarse_parts, turned, *gather(coeffs)],
        )
        got_parts = swap(parts)
        base = run(
            functools.partial(base_kernel, scaled), name + "_base", four(depth + extra), [],
            [VMEM] * 13, [counts, *fields, *got_fields, *parts],
        )
        return base, got_parts

    base, got_parts = correction(False, gaps, got_gaps)
    *first, sums = run(
        first_kernel, "first", four(depth) + four(tall) + [shape(2, columns)], [flat],
        [VMEM] * 10, [counts, operator, *base, *got_parts],
    )
    first, images = first[:PARTNERS], first[PARTNERS:]
    got_images = swap(images)
    first_turned = run(columns_kernel, "columns", shape(PARTNERS, columns, depth), [], [VMEM] * 4, first)
    base, got_parts = correction(True, images, got_images)
    second_turned, sums = run(
        second_kernel, "second", [shape(PARTNERS, columns, depth), shape(rows * cols, 8, columns)],
        [flat] + [pltpu.VMEM((depth, columns), jnp.float32)] * PARTNERS,
        [VMEM] * 19 + [ANY], [counts, operator, sums, *base, *got_parts, *images, *first, first_turned],
    )
    every = lax.all_to_all(sums, ("col", "row"), 0, 0)
    whole = (columns, PARTNERS, depth)
    out = run(
        last_kernel, "last", shape(*whole),
        [pltpu.VMEM(whole, jnp.float32), pltpu.SemaphoreType.DMA((2,))],
        [VMEM] * 3, [every, first_turned, second_turned], out_spec=HBM,
    )
    return out[None, None]


def solution(mesh):
    rows, cols = mesh.shape["row"], mesh.shape["col"]

    def body(*arrays):
        return on_device(rows, cols, *arrays)

    return jax.shard_map(
        body,
        mesh=mesh,
        in_specs=(
            P("row", "col", None, None, None),
            P("row", "col", None, None),
            P("row", "col", None, None),
            P("row", "col", None),
            P("row", "col", None),
        ),
        out_specs=P("row", "col", None, None, None),
        check_vma=False,
    )
```
